512 devices in a mesh: sec: 16 (over x, z_hi, core), elem: 32 (over y, z_lo).
Axes of the slice: x: 4, y: 8, z: 8 (z_hi: 2, z_lo: 4; z = z_hi * 4 + z_lo), core: 2. Of those that a mesh axis runs over, the one named last changes fastest.
Arguments:
- thermal_level_points: float32 [16, 8, 8, 8, 4096], P('sec', None, None, None, 'elem'), may hold values from -6 to 6
- flow_speed_vector: float32 [3, 16, 8, 8, 8, 4096], P(None, 'sec', None, None, None, 'elem'), may hold values from -3 to 3
- thermal_diffusivity_cell: float32 [16, 4096], P('sec', 'elem'), may hold values from 0.3 to 3
- metal_cell_indicator: int32 [16, 4096], P('sec', 'elem'), may hold values 0 or 1
- adjoining_patch: int32 [16, 4096], P('sec', 'elem'), may hold values from 0 to 15, as said below
Outputs:
- temperature_out: float32 [16, 8, 8, 8, 4096], P('sec', None, None, None, 'elem')
The draws below stay inside these ranges and needn't reach their ends.
Inputs may be any that keep to these rules, and one draw needn't show every extreme that they name: adjoining_patch[adjoining_patch[s, e], e] = s and adjoining_patch[s, e] != s: at every chain position the sections are paired; within each aligned block of 128 chain positions a pair of sections shares at most 9 positions, and some pair shares exactly 9.
All inputs are finite; a program needn't handle non-finite values. No bound on the sum of `metal_cell_indicator` on one device may be relied on, other than what follows from the above.
Results may differ from the reference program's by a relative error of at most 0.0001.
Values sent between devices are 32-bit elements; how exact they have to be, the bound alone decides.
A program may use at most 64 MiB of HBM per device.

```python
import math
import jax
import jax.numpy as jnp
import numpy as np
from jax import lax

LINE_POINT_TOTAL = 8
FINE = 11
ELEM_DEV = 128
SWEEPS = 4
STEPS = 2
PATCH_CELLS = 4096
N_SEC = 16


def draw_adjoining_patch(key, part):
    block_count = PATCH_CELLS // ELEM_DEV
    block_keys = jax.random.split(jax.random.fold_in(key, 17), block_count)
    orders = jax.vmap(lambda single_key: jax.random.permutation(single_key, ELEM_DEV))(block_keys)
    mate_code = (orders.astype(jnp.int32) % (N_SEC - 1) + 1).reshape((PATCH_CELLS,))
    sections = jnp.arange(N_SEC, dtype=jnp.int32)
    return jnp.bitwise_xor(sections[:, None], mate_code[None, :]).astype(jnp.int32)


def set_ends(array, stream_key, least, largest):
    place = [jax.random.randint(jax.random.fold_in(stream_key, axis), (), 0, length) for axis, length in enumerate(array.shape)]
    longest = array.shape.index(max(array.shape))
    next_to = place[:longest] + [(place[longest] + 1) % array.shape[longest]] + place[longest + 1:]
    return array.at[tuple(place)].set(least).at[tuple(next_to)].set(largest)


def level_of(rng, shape, cuts, low, top_value):
    def one(position, parts):
        steps = jax.random.uniform(jax.random.fold_in(jax.random.fold_in(rng, 6), position), (parts,), jnp.float32, low / len(cuts), top_value / len(cuts))
        return jnp.repeat(jnp.exp(steps), shape[position] // parts).reshape((-1,) + (1,) * (len(shape) - position - 1))

    factor_of = one(*cuts[0])
    for cut in cuts[1:]:
        factor_of = factor_of * one(*cut)
    return factor_of


def bell_draw(stream_key, dims, spread, most, shards=(), held_as=jnp.bfloat16):
    values = spread * jax.random.normal(stream_key, dims, jnp.float32)
    if shards:
        values = values * level_of(stream_key, dims, shards, -0.22, 0.18)
    return jnp.clip(values, -most, most).astype(held_as)


def setup_inputs(seed: int = 0) -> dict:
    seeds = jax.random.split(jax.random.key(seed), 6)
    return {
        "thermal_level_points": bell_draw(seeds[0], (N_SEC, LINE_POINT_TOTAL, LINE_POINT_TOTAL, LINE_POINT_TOTAL, PATCH_CELLS), 1.0, 6.0, ((0, 16), (4, 32)), jnp.float32),
        "flow_speed_vector": bell_draw(seeds[1], (3, N_SEC, LINE_POINT_TOTAL, LINE_POINT_TOTAL, LINE_POINT_TOTAL, PATCH_CELLS), 0.5, 3.0, ((1, 16), (5, 32)), jnp.float32),
        "thermal_diffusivity_cell": jnp.clip(jnp.exp(math.log(3.0) - 2.3025851 * jax.random.uniform(seeds[2], (N_SEC, PATCH_CELLS), jnp.float32) ** level_of(seeds[2], (N_SEC, PATCH_CELLS), ((0, 16), (1, 32)), -0.2, 0.2)), 0.3, 3.0),
        "metal_cell_indicator": set_ends((jax.random.randint(seeds[3], (N_SEC, PATCH_CELLS), 0, 5) < 1).astype(jnp.int32), jax.random.fold_in(seeds[3], 1), 0, 1),
        "adjoining_patch": draw_adjoining_patch(jax.random.fold_in(seeds[5], 71), 0),
    }


highest = lax.Precision.HIGHEST
time_step = 0.05
relaxation = 0.4
penalty = 30.0


def legendre_pair(order, points):
    previous = points * 0.0 + 1.0
    current = points * 1.0
    for level in range(2, order + 1):
        previous, current = current, ((2 * level - 1) * points * current - (level - 1) * previous) / level
    return current, previous


def make_tables():
    degree = LINE_POINT_TOTAL - 1
    gll_nodes = -np.cos(np.pi * np.arange(LINE_POINT_TOTAL) / degree)
    for repeat in range(100):
        current, previous = legendre_pair(degree, gll_nodes)
        gll_nodes = gll_nodes - (gll_nodes * current - previous) / (LINE_POINT_TOTAL * current)
    values, lower_values = legendre_pair(degree, gll_nodes)
    weights = 2.0 / (degree * (degree + 1) * values ** 2)
    spatial_derivative = np.zeros((LINE_POINT_TOTAL, LINE_POINT_TOTAL))
    for row_index in range(LINE_POINT_TOTAL):
        for column_index in range(LINE_POINT_TOTAL):
            if row_index != column_index:
                spatial_derivative[row_index, column_index] = values[row_index] / (values[column_index] * (gll_nodes[row_index] - gll_nodes[column_index]))
    spatial_derivative[0, 0] = -degree * (degree + 1) / 4.0
    spatial_derivative[-1, -1] = degree * (degree + 1) / 4.0
    fine_nodes = -np.cos(np.pi * (np.arange(FINE) + 0.75) / (FINE + 0.5))
    for repeat in range(100):
        current, previous = legendre_pair(FINE, fine_nodes)
        slope = FINE * (fine_nodes * current - previous) / (fine_nodes * fine_nodes - 1.0)
        fine_nodes = fine_nodes - current / slope
    current, previous = legendre_pair(FINE, fine_nodes)
    slope = FINE * (fine_nodes * current - previous) / (fine_nodes * fine_nodes - 1.0)
    fine_weights = 2.0 / ((1.0 - fine_nodes * fine_nodes) * slope * slope)
    interpolation = np.ones((FINE, LINE_POINT_TOTAL))
    for column_index in range(LINE_POINT_TOTAL):
        for other_index in range(LINE_POINT_TOTAL):
            if other_index != column_index:
                interpolation[:, column_index] *= (fine_nodes - gll_nodes[other_index]) / (gll_nodes[column_index] - gll_nodes[other_index])
    stiffness_1d = spatial_derivative.T @ (weights[:, None] * spatial_derivative)
    return (jnp.asarray(spatial_derivative, jnp.float32), jnp.asarray(interpolation, jnp.float32),
            jnp.asarray(stiffness_1d, jnp.float32), jnp.asarray(weights, jnp.float32),
            jnp.asarray(fine_weights, jnp.float32))


def act_along_coordinate(matrix, grid_values, coordinate_axis_label):
    if coordinate_axis_label == 0:
        return jnp.einsum("qa,sabce->sqbce", matrix, grid_values, precision=highest)
    if coordinate_axis_label == 1:
        return jnp.einsum("qb,sabce->saqce", matrix, grid_values, precision=highest)
    return jnp.einsum("qc,sabce->sabqe", matrix, grid_values, precision=highest)


def lift_fine(matrix, grid_values):
    result = grid_values
    for coordinate_axis_label in range(3):
        result = act_along_coordinate(matrix, result, coordinate_axis_label)
    return result


def point_weights(weights):
    return (weights[None, :, None, None, None], weights[None, None, :, None, None], weights[None, None, None, :, None])


def mass_grid(weights):
    weight_a, weight_b, weight_c = point_weights(weights)
    return weight_a * weight_b * weight_c


def transport_flux(thermal_level_points, flow_speed_vector, liquid_cell_indicator, spectral_matrix_bundle):
    spatial_derivative, interpolation, stiffness_1d, weights, fine_weights = spectral_matrix_bundle
    fluid_grid = liquid_cell_indicator[:, None, None, None, :]
    product_sum = None
    for coordinate_axis_label in range(3):
        slope_vector_values = act_along_coordinate(spatial_derivative, thermal_level_points, coordinate_axis_label)
        term = lift_fine(interpolation, flow_speed_vector[coordinate_axis_label] * fluid_grid) * lift_fine(interpolation, slope_vector_values)
        product_sum = term if coordinate_axis_label == 0 else product_sum + term
    cube = fine_weights[:, None, None] * fine_weights[None, :, None] * fine_weights[None, None, :]
    return lift_fine(interpolation.T, product_sum * cube[None, :, :, :, None])


def stiffness_apply(grid_values, spectral_matrix_bundle):
    stiffness_1d = spectral_matrix_bundle[2]
    weight_a, weight_b, weight_c = point_weights(spectral_matrix_bundle[3])
    return (act_along_coordinate(stiffness_1d, grid_values, 0) * (weight_b * weight_c)
            + act_along_coordinate(stiffness_1d, grid_values, 1) * (weight_a * weight_c)
            + act_along_coordinate(stiffness_1d, grid_values, 2) * (weight_a * weight_b))


def face_terms(grid_values, near_minus, near_plus, far_wall, coefficients, spectral_matrix_bundle):
    coef_left, coef_right, coef_wall = coefficients
    weights = spectral_matrix_bundle[3]
    face_weight = (weights[:, None] * weights[None, :])[None, :, :, None]
    result = jnp.zeros_like(grid_values)
    result = result.at[:, 0].add(coef_left[:, None, None, :] * face_weight * (grid_values[:, 0] - near_plus))
    result = result.at[:, -1].add(coef_right[:, None, None, :] * face_weight * (grid_values[:, -1] - near_minus))
    result = result.at[:, :, :, 0].add(coef_wall[:, None, None, :] * face_weight * (grid_values[:, :, :, 0] - far_wall))
    return result


def diagonal_h(thermal_diffusivity_cell, coefficients, spectral_matrix_bundle):
    coef_left, coef_right, coef_wall = coefficients
    stiffness_1d, weights = spectral_matrix_bundle[2], spectral_matrix_bundle[3]
    weight_a, weight_b, weight_c = point_weights(weights)
    stiff_diag = jnp.diagonal(stiffness_1d)
    k_diag = (stiff_diag[None, :, None, None, None] * weight_b * weight_c
              + weight_a * stiff_diag[None, None, :, None, None] * weight_c
              + weight_a * weight_b * stiff_diag[None, None, None, :, None])
    result = mass_grid(weights) / time_step + thermal_diffusivity_cell[:, None, None, None, :] * k_diag
    face_weight = (weights[:, None] * weights[None, :])[None, :, :, None]
    result = result.at[:, 0].add(coef_left[:, None, None, :] * face_weight)
    result = result.at[:, -1].add(coef_right[:, None, None, :] * face_weight)
    result = result.at[:, :, :, 0].add(coef_wall[:, None, None, :] * face_weight)
    return result


def sweep_update(iterate, right_side, diagonal, faces_part, thermal_diffusivity_cell, spectral_matrix_bundle):
    applied = (mass_grid(spectral_matrix_bundle[3]) / time_step * iterate
               + thermal_diffusivity_cell[:, None, None, None, :] * stiffness_apply(iterate, spectral_matrix_bundle) + faces_part)
    return iterate + relaxation * (right_side - applied) / diagonal


def reference(thermal_level_points, flow_speed_vector, thermal_diffusivity_cell, metal_cell_indicator, adjoining_patch):
    spectral_matrix_bundle = make_tables()
    padded = jnp.pad(thermal_diffusivity_cell, ((0, 0), (1, 1)))
    chain_index = jnp.arange(thermal_diffusivity_cell.shape[1], dtype=jnp.int32)
    coef_right = jnp.where(chain_index < PATCH_CELLS - 1, penalty * (thermal_diffusivity_cell + padded[:, 2:]) * 0.5, 0.0)
    coef_left = jnp.where(chain_index > 0, penalty * (thermal_diffusivity_cell + padded[:, :-2]) * 0.5, 0.0)
    partner_k = jnp.take_along_axis(thermal_diffusivity_cell, adjoining_patch, axis=0)
    partner_solid = jnp.take_along_axis(metal_cell_indicator, adjoining_patch, axis=0)
    coef_wall = jnp.where(metal_cell_indicator != partner_solid, penalty * (thermal_diffusivity_cell + partner_k) * 0.5, 0.0)
    coefficients = (coef_left, coef_right, coef_wall)
    liquid_cell_indicator = 1.0 - metal_cell_indicator.astype(jnp.float32)
    diagonal = diagonal_h(thermal_diffusivity_cell, coefficients, spectral_matrix_bundle)
    moved_velocity = jnp.moveaxis(flow_speed_vector, 1, 0)

    def per_section(section_data):
        temp_section, velocity_section, fluid_section = section_data
        return transport_flux(temp_section[None], velocity_section[:, None], fluid_section[None], spectral_matrix_bundle)[0]

    iteration_snapshot = thermal_level_points
    for step_index in range(STEPS):
        convected = lax.map(per_section, (iteration_snapshot, moved_velocity, liquid_cell_indicator))
        right_side = mass_grid(spectral_matrix_bundle[3]) / time_step * iteration_snapshot - convected
        iterate = iteration_snapshot
        for sweep_index in range(SWEEPS):
            near_minus = jnp.pad(iterate[:, 0], ((0, 0), (0, 0), (0, 0), (0, 1)))[..., 1:]
            near_plus = jnp.pad(iterate[:, -1], ((0, 0), (0, 0), (0, 0), (1, 0)))[..., :-1]
            wall_face = iterate[:, :, :, 0]
            index_grid = jnp.broadcast_to(adjoining_patch[:, None, None, :], wall_face.shape)
            far_wall = jnp.take_along_axis(wall_face, index_grid, axis=0)
            faces_part = face_terms(iterate, near_minus, near_plus, far_wall, coefficients, spectral_matrix_bundle)
            iterate = sweep_update(iterate, right_side, diagonal, faces_part, thermal_diffusivity_cell, spectral_matrix_bundle)
        iteration_snapshot = iterate
    return iteration_snapshot
```

```python
import jax
import jax.numpy as jnp
import numpy as np
from jax import lax
from jax.experimental import pallas as pl
from jax.experimental.pallas import tpu as pltpu
from jax.sharding import PartitionSpec as P

N = 8
FINE = 11
PLANE = N * N
POINTS = N * N * N
LANES = 128
STEPS = 2
SWEEPS = 4
PAIRS = STEPS * SWEEPS // 2
SLOTS = 9
ROWS = 16
INV_DT = 20.0
RELAX = 0.4
PENALTY = 30.0
MESH = pl.DeviceIdType.MESH
HIGHEST = lax.Precision.HIGHEST
F32 = jnp.float32
BF16 = jnp.bfloat16


def legendre_pair(order, points):
    previous = points * 0.0 + 1.0
    current = points * 1.0
    for level in range(2, order + 1):
        previous, current = (
            current,
            ((2 * level - 1) * points * current - (level - 1) * previous) / level,
        )
    return current, previous


def make_tables():
    degree = N - 1
    x = -np.cos(np.pi * np.arange(N) / degree)
    for _ in range(100):
        cur, prev = legendre_pair(degree, x)
        x = x - (x * cur - prev) / (N * cur)
    values, _ = legendre_pair(degree, x)
    w = 2.0 / (degree * (degree + 1) * values**2)
    dm = np.zeros((N, N))
    for i in range(N):
        for j in range(N):
            if i != j:
                dm[i, j] = values[i] / (values[j] * (x[i] - x[j]))
    dm[0, 0] = -degree * (degree + 1) / 4.0
    dm[-1, -1] = degree * (degree + 1) / 4.0
    g = -np.cos(np.pi * (np.arange(FINE) + 0.75) / (FINE + 0.5))
    for _ in range(100):
        cur, prev = legendre_pair(FINE, g)
        slope = FINE * (g * cur - prev) / (g * g - 1.0)
        g = g - cur / slope
    cur, prev = legendre_pair(FINE, g)
    slope = FINE * (g * cur - prev) / (g * g - 1.0)
    v = 2.0 / ((1.0 - g * g) * slope * slope)
    jm = np.ones((FINE, N))
    for j in range(N):
        for i in range(N):
            if i != j:
                jm[:, j] *= (g - x[i]) / (x[j] - x[i])
    km = dm.T @ (w[:, None] * dm)
    return dm, jm, km, w, v


DM, JM, KM, W, V = make_tables()
JD = JM @ DM
LAP = KM / W[:, None]
ADJ = (JM.T * V[None, :]) / W[:, None]
FACE = PENALTY * 0.5 / W[0]


def halves(m):
    hi = np.asarray(m, np.float32).astype(BF16)
    lo = np.asarray(m - hi.astype(np.float64), np.float32).astype(BF16)
    return hi, lo


def stacked(m):
    hi, lo = halves(m)
    return np.concatenate([hi, hi, lo], axis=1)


def pad_to(m, rows, cols):
    out = np.zeros((rows, cols))
    out[: m.shape[0], : m.shape[1]] = m
    return out


def constants():
    planes = [pad_to(np.kron(p, q), LANES, PLANE) for p, q in ((JM, JM), (JD, JM), (JM, JD))]
    lift = stacked(np.concatenate(planes, axis=0))
    fall = stacked(pad_to(np.kron(ADJ, ADJ), PLANE, LANES))
    eye = np.eye(N)
    lap = (
        np.kron(np.kron(LAP, eye), eye)
        + np.kron(np.kron(eye, LAP), eye)
        + np.kron(np.kron(eye, eye), LAP)
    )
    lap_hi, lap_lo = halves(lap)
    diag = np.broadcast_to(np.diagonal(lap)[:, None], (POINTS, LANES)).astype(np.float32)
    return lift, fall, lap_hi, lap_lo, diag


def dot(a, b):
    return lax.dot_general(a, b, (((1,), (0,)), ((), ())), preferred_element_type=F32)


def dot_nt(a, b):
    return lax.dot_general(
        a, b, (((1,), (1,)), ((), ())), precision=HIGHEST, preferred_element_type=F32
    )


def dot_tn(a, b):
    return lax.dot_general(
        a, b, (((0,), (0,)), ((), ())), precision=HIGHEST, preferred_element_type=F32
    )


def split(x):
    hi = x.astype(BF16)
    lo = (x - hi.astype(F32)).astype(BF16)
    return hi, lo


def split3(x):
    hi, lo = split(x)
    return jnp.concatenate([hi, lo, hi], axis=0)


def weighted(coefs, terms):
    total = None
    for c, t in zip(coefs, terms):
        if c == 0.0:
            continue
        total = t * float(c) if total is None else total + t * float(c)
    return total


def up(table, sign, terms):
    even = [terms[a] + terms[7 - a] for a in range(4)]
    odd = [terms[a] - terms[7 - a] for a in range(4)]
    out = [None] * FINE
    for q in range(6):
        ce = [(table[q, a] + table[q, 7 - a]) / 2 for a in range(4)]
        co = [(table[q, a] - table[q, 7 - a]) / 2 for a in range(4)]
        if q == 5:
            out[q] = weighted(ce, even) if sign > 0 else weighted(co, odd)
            continue
        e, o = weighted(ce, even), weighted(co, odd)
        out[q] = e + o
        out[10 - q] = e - o if sign > 0 else o - e
    return out


def down(table, terms):
    even = [terms[q] + terms[10 - q] for q in range(5)] + [terms[5]]
    odd = [terms[q] - terms[10 - q] for q in range(5)]
    out = [None] * N
    for a in range(4):
        ce = [(table[a, q] + table[a, 10 - q]) / 2 for q in range(5)] + [table[a, 5]]
        co = [(table[a, q] - table[a, 10 - q]) / 2 for q in range(5)]
        e, o = weighted(ce, even), weighted(co, odd)
        out[a] = e + o
        out[7 - a] = e - o
    return out


def iota(shape, dim):
    return lax.broadcasted_iota(jnp.int32, shape, dim)


def kernel(
    n_sec, n_elem,
    th, vel, kd, mt, pt, lift, fall, lap_hi, lap_lo, diag,
    out,
    xs, vs, bs, db, gs, dk, ds, lx, tt, uu, zz, pm, ws,
    fx, fv, ha, hb, hc, dcl, dcr, dclh, dcrh, dcw, dcwp, dpcl, dpcr, dhx, dhw, rowp,
    wsend, wrecv, asend, arecv, csend, left, right,
    ws_sem, wr_sem, as_sem, ar_sem, rs_sem, ls_sem, lr_sem, rr_sem,
):
    me = lax.axis_index("sec")
    el = lax.axis_index("elem")
    nxt = lax.rem(el + 1, n_elem)
    prv = lax.rem(el + n_elem - 1, n_elem)

    def sec(d):
        return lax.rem(me + d, n_sec)

    barrier = pltpu.get_barrier_semaphore()
    for d in range(1, n_sec):
        pl.semaphore_signal(barrier, inc=1, device_id={"sec": sec(d), "elem": el}, device_id_type=MESH)
    for d in range(n_sec):
        pl.semaphore_signal(barrier, inc=1, device_id={"sec": sec(d), "elem": nxt}, device_id_type=MESH)
        pl.semaphore_signal(barrier, inc=1, device_id={"sec": sec(d), "elem": prv}, device_id_type=MESH)

    lane = iota((1, LANES), 1)
    k = kd[...]
    solid = mt[...].astype(F32)
    patch = pt[...]
    patch_f = patch.astype(F32)
    first, last = lane == 0, lane == LANES - 1
    has_prev = (jnp.zeros((1, LANES), jnp.int32) + el) > 0
    has_next = (jnp.zeros((1, LANES), jnp.int32) + el) < n_elem - 1
    wall_row = lax.rem(iota((PLANE, LANES), 0), N) == 0

    def at_lane(row, i):
        return jnp.sum(jnp.where(lane == i, row, 0.0), axis=1, keepdims=True)

    mate = lax.rem(patch - me + n_sec, n_sec) - 1
    member = (iota((ROWS, LANES), 0) == mate).astype(F32)
    before = (iota((LANES, LANES), 0) < iota((LANES, LANES), 1)).astype(F32)
    rank = jnp.sum(member * dot(member, before), axis=0, keepdims=True)
    target = mate * ROWS + rank.astype(jnp.int32)
    pm[...] = (iota(pm.shape, 0) == target).astype(F32)
    ws[...] = jnp.zeros(ws.shape, F32)

    clin = jnp.where(first, 0.0, FACE * (k + pltpu.roll(k, 1, 1)))
    crin = jnp.where(last, 0.0, FACE * (k + pltpu.roll(k, LANES - 1, 1)))

    def rolled(v, by):
        return pltpu.roll(v, by, 1)

    def lift_planes(src, base, table):
        res = []
        for p in range(4):
            cols = []
            for i in range(2):
                start = base + (2 * p + i) * PLANE
                if not isinstance(start, int):
                    start = pl.multiple_of(start, PLANE)
                cols.append(split3(src[pl.ds(start, PLANE), :]))
            res.append(dot(table, jnp.concatenate(cols, axis=1)))
        return res

    def velocity(d, c):
        for p, r in enumerate(lift_planes(vel, d * POINTS, lift[0:LANES, :])):
            for i in range(2):
                tt[d, 2 * p + i] = r[:, i * LANES : (i + 1) * LANES]
        return c

    lax.fori_loop(0, 3, velocity, 0)
    fluid = jnp.broadcast_to(1.0 - solid, (8, LANES))

    def velocity_up(i, c):
        d = i // 16
        rows = pl.ds(pl.multiple_of((i % 16) * 8, 8), 8)
        lifted = up(JM, 1, [tt[d, a, rows, :] for a in range(N)])
        for q in range(FINE):
            uu[d, q, rows, :] = lifted[q] * fluid
        return c

    lax.fori_loop(0, 48, velocity_up, 0)

    def convect():
        for p, r in enumerate(lift_planes(xs, 0, lift[...])):
            for i in range(2):
                for d in range(3):
                    tt[d, 2 * p + i] = r[d * LANES : (d + 1) * LANES, i * LANES : (i + 1) * LANES]

        def product(i, c):
            rows = pl.ds(pl.multiple_of(i * 8, 8), 8)
            total = None
            for d, (table, sign) in enumerate(((JD, -1), (JM, 1), (JM, 1))):
                lifted = up(table, sign, [tt[d, a, rows, :] for a in range(N)])
                terms = [lifted[q] * uu[d, q, rows, :] for q in range(FINE)]
                total = terms if total is None else [x + y for x, y in zip(total, terms)]
            for a, z in enumerate(down(ADJ, total)):
                zz[a, rows, :] = z
            return c

        lax.fori_loop(0, 16, product, 0)
        for p in range(4):
            r = dot(fall[...], jnp.concatenate([split3(zz[2 * p]), split3(zz[2 * p + 1])], axis=1))
            for i in range(2):
                rows = slice((2 * p + i) * PLANE, (2 * p + i + 1) * PLANE)
                bs[rows, :] = INV_DT * xs[rows, :] - r[:, i * LANES : (i + 1) * LANES]

    def laplace():
        hi, lo = split(xs[...])
        return dot(lap_hi[...], hi) + dot(lap_hi[...], lo) + dot(lap_lo[...], hi)

    TOP = slice(0, PLANE)
    END = slice(POINTS - PLANE, POINTS)

    def local(applied):
        vs[...] = gs[...] * xs[...] + db[...] - dk[...] * applied
        vs[TOP, :] += dcl[...] * rolled(xs[END, :], 1)
        vs[END, :] += dcr[...] * rolled(xs[TOP, :], LANES - 1)

    sel_last = jnp.where((iota((8, LANES), 0) == 0) & (iota((8, LANES), 1) == LANES - 1), 1.0, 0.0)
    sel_first = jnp.where((iota((8, LANES), 0) == 0) & (iota((8, LANES), 1) == 0), 1.0, 0.0)
    full_row = iota((LANES, LANES), 0)

    def pack_and_send(m, second):
        walls = jnp.concatenate([xs[0:POINTS:N, :], second[0:POINTS:N, :]], axis=0)
        packed = dot_nt(pm[...], walls)
        for j in range(n_sec - 1):
            wsend[m, j] = packed[j * ROWS : j * ROWS + SLOTS]
        for j in range(n_sec - 1):
            to = {"sec": sec(j + 1), "elem": el}
            pltpu.make_async_remote_copy(
                wsend.at[m, j], wrecv.at[m, n_sec - 2 - j], ws_sem.at[m], wr_sem.at[m],
                device_id=to, device_id_type=MESH,
            ).start()
        csend[m, 0, 0:1] = dot_nt(sel_last, jnp.concatenate([xs[END, :], second[END, :]], axis=0))[0:1]
        csend[m, 1, 0:1] = dot_nt(sel_first, jnp.concatenate([xs[TOP, :], second[TOP, :]], axis=0))[0:1]
        for d in range(n_sec):
            pltpu.make_async_remote_copy(
                csend.at[m, 0], left.at[m, me], rs_sem.at[m], lr_sem.at[m],
                device_id={"sec": sec(d), "elem": nxt}, device_id_type=MESH,
            ).start()
            pltpu.make_async_remote_copy(
                csend.at[m, 1], right.at[m, me], ls_sem.at[m], rr_sem.at[m],
                device_id={"sec": sec(d), "elem": prv}, device_id_type=MESH,
            ).start()

    xs[...] = th[...]
    convect()
    lx[...] = laplace()
    vs[...] = bs[...] - INV_DT * xs[...] - k * lx[...]
    vs[TOP, :] += clin * (rolled(xs[END, :], 1) - xs[TOP, :])
    vs[END, :] += crin * (rolled(xs[TOP, :], LANES - 1) - xs[END, :])

    traits = jnp.where(full_row == 0, k, 0.0)
    traits = jnp.where(full_row == 1, solid, traits)
    traits = jnp.where(full_row == 2, patch_f, traits)
    traits = jnp.where(full_row == 3, clin, traits)
    traits = jnp.where(full_row == 4, crin, traits)
    packed_traits = dot_nt(pm[...], traits)
    for j in range(n_sec - 1):
        asend[j] = packed_traits[j * ROWS : j * ROWS + SLOTS]
    csend[0, 0, 1:2] = dot_nt(sel_last, traits)[0:1]
    csend[0, 1, 1:2] = dot_nt(sel_first, traits)[0:1]
    for m in range(1, PAIRS):
        for i in range(2):
            csend[m, i, 1:2] = jnp.zeros((1, LANES), F32)

    pl.semaphore_wait(barrier, 3 * n_sec - 1)
    for j in range(n_sec - 1):
        pltpu.make_async_remote_copy(
            asend.at[j], arecv.at[n_sec - 2 - j], as_sem.at[0], ar_sem.at[0],
            device_id={"sec": sec(j + 1), "elem": el}, device_id_type=MESH,
        ).start()
    pack_and_send(0, vs)

    row8 = iota((8, LANES), 0)
    lane8 = iota((8, LANES), 1)

    def ends(i):
        return jnp.where(((row8 == i) & (lane8 == 0)) | ((row8 == i + 1) & (lane8 == LANES - 1)), 1.0, 0.0)

    end_map = jnp.concatenate([ends(0), ends(2), ends(4)], axis=1)

    def pick(ref, m, which, r):
        total = jnp.zeros((1, LANES), F32)
        for q in range(n_sec):
            total = jnp.where(which == float(q), ref[m, q, r : r + 1, :], total)
        return total

    def unpack(ref_rows):
        for j in range(n_sec - 1):
            ws[j * ROWS : j * ROWS + SLOTS, :] = ref_rows(j)
        return dot_tn(ws[...], pm[...])

    def both(at_first, at_last):
        return jnp.where(first, at_first, jnp.where(last, at_last, 0.0))

    def pair(m, c):
        pltpu.make_async_copy(left.at[m], left.at[m], lr_sem.at[m]).wait()
        pltpu.make_async_copy(right.at[m], right.at[m], rr_sem.at[m]).wait()
        pltpu.make_async_copy(wrecv.at[m], wrecv.at[m], wr_sem.at[m]).wait()
        far = unpack(lambda j: wrecv[m, j])
        fx[...] = far[0:PLANE]
        fv[...] = far[PLANE : 2 * PLANE]

        @pl.when(m == 0)
        def _():
            rowp[0] = jnp.broadcast_to(at_lane(patch_f, 0), (1, LANES))
            rowp[1] = jnp.broadcast_to(at_lane(patch_f, LANES - 1), (1, LANES))
            rowp[2] = jnp.broadcast_to(at_lane(left[0, me, 1:2, :], 2), (1, LANES))
            rowp[3] = jnp.broadcast_to(at_lane(right[0, me, 1:2, :], 2), (1, LANES))

        rows = [
            pick(left, m, rowp[0], 0), pick(right, m, rowp[1], 0),
            left[m, me, 0:1, :], right[m, me, 0:1, :],
            pick(left, m, rowp[2], 0), pick(right, m, rowp[3], 0),
        ]
        stack = jnp.zeros((8, LANES), F32)
        for i, r in enumerate(rows):
            stack = jnp.where(row8 == i, r, stack)
        ended = dot_tn(stack, end_map)
        ha[...] = ended[:, 0:LANES]
        hb[...] = ended[:, LANES : 2 * LANES]
        hc[...] = ended[:, 2 * LANES : 3 * LANES]

        @pl.when(m == 0)
        def _():
            pltpu.make_async_copy(arecv, arecv, ar_sem.at[0]).wait()
            theirs = unpack(lambda j: arecv[j])
            kp, sp = theirs[0:1], theirs[1:2]
            clp, crp = theirs[3:4], theirs[4:5]
            own_left, own_right = left[0, me, 1:2, :], right[0, me, 1:2, :]
            wall_left, wall_right = pick(left, 0, rowp[0], 1), pick(right, 0, rowp[1], 1)
            far_left, far_right = pick(left, 0, rowp[2], 1), pick(right, 0, rowp[3], 1)
            kg = both(at_lane(own_left, 0), at_lane(own_right, 0))
            sg = both(at_lane(own_left, 1), at_lane(own_right, 1))
            ka = both(at_lane(wall_left, 0), at_lane(wall_right, 0))
            kf = both(at_lane(far_left, 0), at_lane(far_right, 0))
            sf = both(at_lane(far_left, 1), at_lane(far_right, 1))
            at_start, at_end = first & has_prev, last & has_next
            clx = jnp.where(at_start, FACE * (k + kg), 0.0)
            crx = jnp.where(at_end, FACE * (k + kg), 0.0)
            cw = jnp.where(solid != sp, FACE * (k + kp), 0.0)
            cwm = jnp.where(wall_row, cw, 0.0)
            for a in range(N):
                rows_a = slice(a * PLANE, (a + 1) * PLANE)
                extra = cwm + INV_DT
                if a == 0:
                    extra = extra + (clin + clx)
                if a == N - 1:
                    extra = extra + (crin + crx)
                d = RELAX / (extra + k * diag[rows_a, :])
                ds[rows_a, :] = d
                gs[rows_a, :] = 1.0 - d * extra
                dk[rows_a, :] = d * k
                db[rows_a, :] = d * bs[rows_a, :]
            dcl[...] = ds[TOP, :] * clin
            dclh[...] = ds[TOP, :] * clx
            dcr[...] = ds[END, :] * crin
            dcrh[...] = ds[END, :] * crx
            dcw[...] = ds[0:POINTS:N, :] * cw
            clxp = jnp.where(at_start, FACE * (kp + ka), 0.0)
            crxp = jnp.where(at_end, FACE * (kp + ka), 0.0)
            line = iota((PLANE, LANES), 0)
            outer = cw + jnp.where(line < N, clxp, 0.0) + jnp.where(line >= PLANE - N, crxp, 0.0)
            inner = jnp.where(line < N, clp, 0.0) + jnp.where(line >= PLANE - N, crp, 0.0)
            dp = RELAX / (INV_DT + kp * diag[0:POINTS:N, :] + outer + inner)
            fv[...] = fx[...] + dp * (fv[...] - outer * fx[...])
            dcwp[...] = dp * cw
            dpcl[...] = dp[0:N] * clxp
            dpcr[...] = dp[PLANE - N : PLANE] * crxp
            cxg = clx + crx
            cwg = jnp.where(wall_row, jnp.where(sg != sf, FACE * (kg + kf), 0.0), 0.0)
            dg = RELAX / (INV_DT + kg * diag[TOP, :] + cxg + cwg)
            hb[PLANE : 2 * PLANE, :] = hb[TOP, :] + dg * (hb[PLANE : 2 * PLANE, :] - (cxg + cwg) * hb[TOP, :])
            dhx[...] = dg * cxg
            dhw[...] = dg * cwg
            local(lx[...])

        face = xs[0:POINTS:N, :]
        edge = ha[0:PLANE:N, :]
        fv[...] += dcwp[...] * face
        fv[0:N, :] += dpcl[...] * edge
        fv[PLANE - N : PLANE, :] += dpcr[...] * edge
        mine = jnp.where(first, xs[TOP, :], xs[END, :])
        later = hb[PLANE : 2 * PLANE, :] + dhx[...] * mine + dhw[...] * hc[0:PLANE, :]

        def finish(wall, halo):
            xs[...] = vs[...]
            xs[TOP, :] += dclh[...] * halo
            xs[END, :] += dcrh[...] * halo
            xs[0:POINTS:N, :] += dcw[...] * wall

        finish(fx[...], hb[TOP, :])
        local(laplace())
        finish(fv[...], later)

        @pl.when(m == SWEEPS // 2 - 1)
        def _():
            convect()
            db[...] = ds[...] * bs[...]

        @pl.when(m < PAIRS - 1)
        def _():
            local(laplace())
            pack_and_send(m + 1, vs)

        return c

    lax.fori_loop(0, PAIRS, pair, 0)
    out[...] = xs[...]

    pltpu.make_async_copy(asend, asend, as_sem.at[0]).wait()
    for m in range(PAIRS):
        pltpu.make_async_copy(wsend.at[m], wsend.at[m], ws_sem.at[m]).wait()
        pltpu.make_async_copy(left.at[m], left.at[m], rs_sem.at[m]).wait()
        pltpu.make_async_copy(right.at[m], right.at[m], ls_sem.at[m]).wait()


def body(n_sec, n_elem, theta, flow, conduct, metal, patch):
    consts = constants()
    vmem = pl.BlockSpec(memory_space=pltpu.VMEM)
    field = pltpu.VMEM((POINTS, LANES), F32)
    plane = pltpu.VMEM((PLANE, LANES), F32)
    edge = pltpu.VMEM((N, LANES), F32)
    double = pltpu.VMEM((2 * PLANE, LANES), F32)
    peers = n_sec - 1
    dma = pltpu.SemaphoreType.DMA
    result = pl.pallas_call(
        lambda *refs: kernel(n_sec, n_elem, *refs),
        out_shape=jax.ShapeDtypeStruct((POINTS, LANES), F32),
        in_specs=[vmem] * 10,
        out_specs=vmem,
        scratch_shapes=[field] * 8
        + [
            pltpu.VMEM((3, N, LANES, LANES), F32),
            pltpu.VMEM((3, FINE, LANES, LANES), F32),
            pltpu.VMEM((N, LANES, LANES), F32),
            pltpu.VMEM((peers * ROWS, LANES), F32),
            pltpu.VMEM((peers * ROWS, LANES), F32),
        ]
        + [plane] * 2 + [double] * 3 + [plane] * 6 + [edge] * 2 + [plane] * 2
        + [
            pltpu.VMEM((4, 1, LANES), F32),
            pltpu.VMEM((PAIRS, peers, SLOTS, LANES), F32),
            pltpu.VMEM((PAIRS, peers, SLOTS, LANES), F32),
            pltpu.VMEM((peers, SLOTS, LANES), F32),
            pltpu.VMEM((peers, SLOTS, LANES), F32),
            pltpu.VMEM((PAIRS, 2, 2, LANES), F32),
            pltpu.VMEM((PAIRS, n_sec, 2, LANES), F32),
            pltpu.VMEM((PAIRS, n_sec, 2, LANES), F32),
        ]
        + [dma((PAIRS,)), dma((PAIRS,)), dma((1,)), dma((1,))]
        + [dma((PAIRS,))] * 4,
        compiler_params=pltpu.CompilerParams(collective_id=0, has_side_effects=True),
    )(
        theta.reshape(POINTS, LANES),
        flow.reshape(3 * POINTS, LANES),
        conduct, metal, patch,
        *[jnp.asarray(c) for c in consts],
    )
    return result.reshape(theta.shape)


def solution(mesh):
    n_sec, n_elem = mesh.shape["sec"], mesh.shape["elem"]
    return jax.shard_map(
        lambda *args: body(n_sec, n_elem, *args),
        mesh=mesh,
        in_specs=(
            P("sec", None, None, None, "elem"),
            P(None, "sec", None, None, None, "elem"),
            P("sec", "elem"),
            P("sec", "elem"),
            P("sec", "elem"),
        ),
        out_specs=P("sec", None, None, None, "elem"),
        check_vma=False,
    )
```

```python
import jax
import jax.numpy as jnp
import numpy as np
from jax import lax
from jax.experimental import pallas as pl
from jax.experimental.pallas import tpu as pltpu
from jax.sharding import PartitionSpec as P

N = 8
FINE = 11
PLANE = N * N
POINTS = N * N * N
LANES = 128
STEPS = 2
SWEEPS = 4
PAIRS = STEPS * SWEEPS // 2
HALF = 5
ROWS = 8
INV_DT = 20.0
RELAX = 0.4
PENALTY = 30.0
MESH = pl.DeviceIdType.MESH
HIGHEST = lax.Precision.HIGHEST
F32 = jnp.float32
BF16 = jnp.bfloat16


def legendre_pair(order, points):
    previous = points * 0.0 + 1.0
    current = points * 1.0
    for level in range(2, order + 1):
        previous, current = (
            current,
            ((2 * level - 1) * points * current - (level - 1) * previous) / level,
        )
    return current, previous


def make_tables():
    degree = N - 1
    x = -np.cos(np.pi * np.arange(N) / degree)
    for _ in range(100):
        cur, prev = legendre_pair(degree, x)
        x = x - (x * cur - prev) / (N * cur)
    values, _ = legendre_pair(degree, x)
    w = 2.0 / (degree * (degree + 1) * values**2)
    dm = np.zeros((N, N))
    for i in range(N):
        for j in range(N):
            if i != j:
                dm[i, j] = values[i] / (values[j] * (x[i] - x[j]))
    dm[0, 0] = -degree * (degree + 1) / 4.0
    dm[-1, -1] = degree * (degree + 1) / 4.0
    g = -np.cos(np.pi * (np.arange(FINE) + 0.75) / (FINE + 0.5))
    for _ in range(100):
        cur, prev = legendre_pair(FINE, g)
        slope = FINE * (g * cur - prev) / (g * g - 1.0)
        g = g - cur / slope
    cur, prev = legendre_pair(FINE, g)
    slope = FINE * (g * cur - prev) / (g * g - 1.0)
    v = 2.0 / ((1.0 - g * g) * slope * slope)
    jm = np.ones((FINE, N))
    for j in range(N):
        for i in range(N):
            if i != j:
                jm[:, j] *= (g - x[i]) / (x[j] - x[i])
    km = dm.T @ (w[:, None] * dm)
    return dm, jm, km, w, v


DM, JM, KM, W, V = make_tables()
JD = JM @ DM
LAP = KM / W[:, None]
ADJ = (JM.T * V[None, :]) / W[:, None]
FACE = PENALTY * 0.5 / W[0]


def halves(m):
    hi = np.asarray(m, np.float32).astype(BF16)
    lo = np.asarray(m - hi.astype(np.float64), np.float32).astype(BF16)
    return hi, lo


def stacked(m):
    hi, lo = halves(m)
    return np.concatenate([hi, hi, lo], axis=1)


def pad_to(m, rows, cols):
    out = np.zeros((rows, cols))
    out[: m.shape[0], : m.shape[1]] = m
    return out


def constants():
    planes = [pad_to(np.kron(p, q), LANES, PLANE) for p, q in ((JM, JM), (JD, JM), (JM, JD))]
    lift = stacked(np.concatenate(planes, axis=0))
    fall = stacked(pad_to(np.kron(ADJ, ADJ), PLANE, LANES))
    eye = np.eye(N)
    flat = np.kron(LAP, eye) + np.kron(eye, LAP)
    main = np.diagonal(LAP)
    diag = main[:, None] + np.diagonal(flat)[None, :]
    diag = np.broadcast_to(diag.reshape(POINTS, 1), (POINTS, LANES)).astype(np.float32)
    return lift, fall, stacked(flat), diag


def dot(a, b):
    return lax.dot_general(a, b, (((1,), (0,)), ((), ())), preferred_element_type=F32)


def dot_nt(a, b):
    return lax.dot_general(a, b, (((1,), (1,)), ((), ())), preferred_element_type=F32)


def split(x):
    hi = x.astype(BF16)
    lo = (x - hi.astype(F32)).astype(BF16)
    return hi, lo


def split3(x):
    hi, lo = split(x)
    return jnp.concatenate([hi, lo, hi], axis=0)


def split_rows(x):
    hi = x.astype(BF16)
    rest = x - hi.astype(F32)
    mid = rest.astype(BF16)
    low = (rest - mid.astype(F32)).astype(BF16)
    return jnp.concatenate([hi.astype(F32), mid.astype(F32), low.astype(F32)], axis=0)


def weighted(coefs, terms):
    total = None
    for c, t in zip(coefs, terms):
        if c == 0.0:
            continue
        total = t * float(c) if total is None else total + t * float(c)
    return total


def up(table, sign, terms):
    even = [terms[a] + terms[7 - a] for a in range(4)]
    odd = [terms[a] - terms[7 - a] for a in range(4)]
    out = [None] * FINE
    for q in range(6):
        ce = [(table[q, a] + table[q, 7 - a]) / 2 for a in range(4)]
        co = [(table[q, a] - table[q, 7 - a]) / 2 for a in range(4)]
        if q == 5:
            out[q] = weighted(ce, even) if sign > 0 else weighted(co, odd)
            continue
        e, o = weighted(ce, even), weighted(co, odd)
        out[q] = e + o
        out[10 - q] = e - o if sign > 0 else o - e
    return out


def across(table, terms):
    even = [terms[j] + terms[7 - j] for j in range(4)]
    odd = [terms[j] - terms[7 - j] for j in range(4)]
    out = [None] * N
    for i in range(4):
        e = weighted([(table[i, j] + table[i, 7 - j]) / 2 for j in range(4)], even)
        o = weighted([(table[i, j] - table[i, 7 - j]) / 2 for j in range(4)], odd)
        out[i] = e + o
        out[7 - i] = e - o
    return out


def down(table, terms):
    even = [terms[q] + terms[10 - q] for q in range(5)] + [terms[5]]
    odd = [terms[q] - terms[10 - q] for q in range(5)]
    out = [None] * N
    for a in range(4):
        ce = [(table[a, q] + table[a, 10 - q]) / 2 for q in range(5)] + [table[a, 5]]
        co = [(table[a, q] - table[a, 10 - q]) / 2 for q in range(5)]
        e, o = weighted(ce, even), weighted(co, odd)
        out[a] = e + o
        out[7 - a] = e - o
    return out


def iota(shape, dim):
    return lax.broadcasted_iota(jnp.int32, shape, dim)


def kernel(
    n_sec, n_elem,
    th, vel, kd, mt, pt, lift, fall, flat, diag,
    out,
    xs, vs, bs, db, gs, dk, ds, lx, tt, uu, zz, pm, ws,
    far, later, pmul, hmul, dcl, dcr, dclh, dcrh, dcw, dcwp, dpcl, dpcr, dhx, dhw, hx, rowp,
    wxs, wxr, wvs, wvr, asend, arecv, cxs, cvs, leftx, rightx, leftv, rightv,
    wxs_sem, wxr_sem, wvs_sem, wvr_sem, as_sem, ar_sem,
    rx_sem, lx_sem, rv_sem, lv_sem, lxr_sem, rxr_sem, lvr_sem, rvr_sem,
):
    me = lax.axis_index("sec")
    el = lax.axis_index("elem")
    nxt = lax.rem(el + 1, n_elem)
    prv = lax.rem(el + n_elem - 1, n_elem)
    peers = n_sec - 1
    TOP = slice(0, PLANE)
    END = slice(POINTS - PLANE, POINTS)
    WALL = slice(0, POINTS, N)

    def sec(d):
        return lax.rem(me + d, n_sec)

    def remote(src, dst, send_sem, recv_sem, to_sec, to_elem):
        pltpu.make_async_remote_copy(
            src, dst, send_sem, recv_sem,
            device_id={"sec": to_sec, "elem": to_elem}, device_id_type=MESH,
        ).start()

    def wait(ref, sem):
        pltpu.make_async_copy(ref, ref, sem).wait()

    barrier = pltpu.get_barrier_semaphore()
    for d in range(n_sec):
        for to in (el, nxt, prv) if d else (nxt, prv):
            pl.semaphore_signal(barrier, inc=1, device_id={"sec": sec(d), "elem": to}, device_id_type=MESH)

    lane = lax.broadcasted_iota(jnp.int32, (1, LANES), 1)
    k = kd[...]
    solid = mt[...].astype(F32)
    patch = pt[...]
    patch_f = patch.astype(F32)
    first, last = lane == 0, lane == LANES - 1
    has_prev = (jnp.zeros((1, LANES), jnp.int32) + el) > 0
    has_next = (jnp.zeros((1, LANES), jnp.int32) + el) < n_elem - 1
    wall_row = lax.rem(iota((PLANE, LANES), 0), N) == 0

    def at_lane(row, i):
        return jnp.sum(jnp.where(lane == i, row, 0.0), axis=1, keepdims=True)

    def rolled(v, by):
        return pltpu.roll(v, by, 1)

    mate = lax.rem(patch - me + n_sec, n_sec) - 1
    member = (iota((16, LANES), 0) == mate).astype(F32)
    before = (iota((LANES, LANES), 0) < iota((LANES, LANES), 1)).astype(F32)
    rank = jnp.sum(member * dot(member, before), axis=0, keepdims=True).astype(jnp.int32)
    slot = iota((LANES, LANES), 0)
    low_slot = ((slot == mate * ROWS + rank) & (rank < HALF)).astype(F32)
    high_slot = ((slot == mate * ROWS + rank - HALF) & (rank >= HALF)).astype(F32)
    pm[...] = jnp.concatenate([low_slot, high_slot], axis=1).astype(BF16)
    ws[...] = jnp.zeros(ws.shape, F32)

    def pack(face):
        total = None
        for piece in split(face):
            none = jnp.zeros_like(piece)
            both = jnp.concatenate(
                [jnp.concatenate([piece, none], axis=1), jnp.concatenate([none, piece], axis=1)], axis=0
            )
            part = dot_nt(pm[...], both)
            total = part if total is None else total + part
        return total

    def unpack(rows):
        for j in range(peers):
            ws[j * ROWS : j * ROWS + HALF, :] = rows[j]
        hi, lo = split(jnp.transpose(ws[...]))
        both = dot(hi, pm[...]) + dot(lo, pm[...])
        return both[0:PLANE, 0:LANES] + both[PLANE : 2 * PLANE, LANES : 2 * LANES]

    clin = jnp.where(first, 0.0, FACE * (k + rolled(k, 1)))
    crin = jnp.where(last, 0.0, FACE * (k + rolled(k, LANES - 1)))

    def lift_planes(src, base, table):
        res = []
        for p in range(4):
            cols = []
            for i in range(2):
                at = base + (2 * p + i) * PLANE
                if not isinstance(at, int):
                    at = pl.multiple_of(at, PLANE)
                cols.append(split3(src[pl.ds(at, PLANE), :]))
            res.append(dot(table, jnp.concatenate(cols, axis=1)))
        return res

    def velocity(d, c):
        for p, r in enumerate(lift_planes(vel, d * POINTS, lift[0:LANES, :])):
            for i in range(2):
                tt[d, 2 * p + i] = r[:, i * LANES : (i + 1) * LANES]
        return c

    lax.fori_loop(0, 3, velocity, 0)
    fluid = jnp.broadcast_to(1.0 - solid, (8, LANES))

    def velocity_up(i, c):
        d = i // 16
        rows = pl.ds(pl.multiple_of((i % 16) * 8, 8), 8)
        lifted = up(JM, 1, [tt[d, a, rows, :] for a in range(N)])
        for q in range(FINE):
            uu[d, q, rows, :] = lifted[q] * fluid
        return c

    lax.fori_loop(0, 48, velocity_up, 0)

    def convect():
        for p, r in enumerate(lift_planes(xs, 0, lift[...])):
            for i in range(2):
                for d in range(3):
                    tt[d, 2 * p + i] = r[d * LANES : (d + 1) * LANES, i * LANES : (i + 1) * LANES]

        def product(i, c):
            rows = pl.ds(pl.multiple_of(i * 8, 8), 8)
            total = None
            for d, (table, sign) in enumerate(((JD, -1), (JM, 1), (JM, 1))):
                lifted = up(table, sign, [tt[d, a, rows, :] for a in range(N)])
                terms = [lifted[q] * uu[d, q, rows, :] for q in range(FINE)]
                total = terms if total is None else [x + y for x, y in zip(total, terms)]
            for a, z in enumerate(down(ADJ, total)):
                zz[a, rows, :] = z
            return c

        lax.fori_loop(0, 16, product, 0)
        for p in range(4):
            r = dot(fall[...], jnp.concatenate([split3(zz[2 * p]), split3(zz[2 * p + 1])], axis=1))
            for i in range(2):
                rows = slice((2 * p + i) * PLANE, (2 * p + i + 1) * PLANE)
                bs[rows, :] = INV_DT * xs[rows, :] - r[:, i * LANES : (i + 1) * LANES]

    def laplace(write):
        for p, r in enumerate(lift_planes(xs, 0, flat[...])):
            for i in range(2):
                at = (2 * p + i) * PLANE
                lx[at : at + PLANE, :] = r[:, i * LANES : (i + 1) * LANES]
        for g in range(8):
            rows = [slice(a * PLANE + 8 * g, a * PLANE + 8 * g + 8) for a in range(N)]
            along = across(LAP, [xs[r, :] for r in rows])
            for r, v in zip(rows, along):
                write(r, v + lx[r, :])

    def local():
        def write(r, v):
            vs[r, :] = gs[r, :] * xs[r, :] + db[r, :] - dk[r, :] * v

        laplace(write)
        vs[TOP, :] += dcl[...] * rolled(xs[END, :], 1)
        vs[END, :] += dcr[...] * rolled(xs[TOP, :], LANES - 1)

    corner = iota((16, LANES), 0)
    corner_lane = iota((16, LANES), 1)
    sel_last = jnp.where((corner == 0) & (corner_lane == LANES - 1), 1.0, 0.0).astype(BF16)
    sel_first = jnp.where((corner == 0) & (corner_lane == 0), 1.0, 0.0).astype(BF16)

    def line(sel, plane):
        hi, lo = split(plane)
        both = jnp.concatenate([hi, lo], axis=0)
        r = dot_nt(sel, both)[0:1]
        return r + rolled(r, PLANE)

    def send_x(m):
        packed = pack(xs[WALL, :])
        for j in range(peers):
            wxs[m, j] = packed[j * ROWS : j * ROWS + HALF]
        for j in range(peers):
            remote(wxs.at[m, j], wxr.at[m, peers - 1 - j], wxs_sem.at[m], wxr_sem.at[m], sec(j + 1), el)
        cxs[m, 0, 0:1] = line(sel_last, xs[END, :])
        cxs[m, 1, 0:1] = line(sel_first, xs[TOP, :])
        for d in range(n_sec):
            remote(cxs.at[m, 0], leftx.at[m, me], rx_sem.at[m], lxr_sem.at[m], sec(d), nxt)
            remote(cxs.at[m, 1], rightx.at[m, me], lx_sem.at[m], rxr_sem.at[m], sec(d), prv)

    def send_v(m):
        packed = pack(vs[WALL, :])
        for j in range(peers):
            wvs[m, j] = packed[j * ROWS : j * ROWS + HALF]
        for j in range(peers):
            remote(wvs.at[m, j], wvr.at[m, peers - 1 - j], wvs_sem.at[m], wvr_sem.at[m], sec(j + 1), el)
        cvs[m, 0] = line(sel_last, vs[END, :])
        cvs[m, 1] = line(sel_first, vs[TOP, :])
        remote(cvs.at[m, 0], leftv.at[m], rv_sem.at[m], lvr_sem.at[m], me, nxt)
        remote(cvs.at[m, 1], rightv.at[m], lv_sem.at[m], rvr_sem.at[m], me, prv)

    xs[...] = th[...]
    full_row = iota((PLANE, LANES), 0)
    traits = jnp.where(full_row == 0, k, 0.0)
    traits = jnp.where(full_row == 1, solid, traits)
    traits = jnp.where(full_row == 2, patch_f, traits)
    traits = jnp.where(full_row == 3, clin, traits)
    traits = jnp.where(full_row == 4, crin, traits)
    packed_traits = pack(traits)
    for j in range(peers):
        asend[j] = packed_traits[j * ROWS : j * ROWS + HALF]
    cxs[0, 0, 1:2] = line(sel_last, traits)
    cxs[0, 1, 1:2] = line(sel_first, traits)
    for m in range(1, PAIRS):
        for i in range(2):
            cxs[m, i, 1:2] = jnp.zeros((1, LANES), F32)

    pl.semaphore_wait(barrier, 3 * n_sec - 1)
    send_x(0)
    for j in range(peers):
        remote(asend.at[j], arecv.at[peers - 1 - j], as_sem.at[0], ar_sem.at[0], sec(j + 1), el)

    convect()

    def residual(r, v):
        vs[r, :] = bs[r, :] - INV_DT * xs[r, :] - k * v

    laplace(residual)
    vs[TOP, :] += clin * (rolled(xs[END, :], 1) - xs[TOP, :])
    vs[END, :] += crin * (rolled(xs[TOP, :], LANES - 1) - xs[END, :])
    send_v(0)

    row8 = iota((8, LANES), 0)
    lane8 = iota((8, LANES), 1)

    def ends(i):
        return jnp.where(((row8 == i) & (lane8 == 0)) | ((row8 == i + 1) & (lane8 == LANES - 1)), 1.0, 0.0)

    def tripled(m):
        return jnp.concatenate([m] * 3, axis=0).astype(BF16)

    end_map = tripled(jnp.concatenate([ends(0), ends(2), ends(4)], axis=1))

    def columns(rows, table):
        stack = jnp.zeros((8, LANES), F32)
        for i, r in enumerate(rows):
            stack = jnp.where(row8 == i, r, stack)
        return dot(jnp.transpose(split_rows(stack)).astype(BF16)[0:PLANE], table)

    def pick(ref, m, which, r):
        total = jnp.zeros((1, LANES), F32)
        for q in range(n_sec):
            total = jnp.where(which == float(q), ref[m, q, r : r + 1, :], total)
        return total

    def both(at_first, at_last):
        return jnp.where(first, at_first, jnp.where(last, at_last, 0.0))

    def finish(wall, halo):
        xs[...] = vs[...]
        xs[TOP, :] += dclh[...] * halo
        xs[END, :] += dcrh[...] * halo
        xs[WALL, :] += dcw[...] * wall

    def pair(m, c):
        wait(leftx.at[m], lxr_sem.at[m])
        wait(rightx.at[m], rxr_sem.at[m])
        wait(wxr.at[m], wxr_sem.at[m])
        fx = unpack([wxr[m, j] for j in range(peers)])

        @pl.when(m == 0)
        def _():
            rowp[0] = jnp.broadcast_to(at_lane(patch_f, 0), (1, LANES))
            rowp[1] = jnp.broadcast_to(at_lane(patch_f, LANES - 1), (1, LANES))
            rowp[2] = jnp.broadcast_to(at_lane(leftx[0, me, 1:2, :], 2), (1, LANES))
            rowp[3] = jnp.broadcast_to(at_lane(rightx[0, me, 1:2, :], 2), (1, LANES))

        ended = columns(
            [
                pick(leftx, m, rowp[0], 0), pick(rightx, m, rowp[1], 0),
                leftx[m, me, 0:1, :], rightx[m, me, 0:1, :],
                pick(leftx, m, rowp[2], 0), pick(rightx, m, rowp[3], 0),
            ],
            end_map,
        )
        hx[...] = ended[:, 0:LANES]
        hb = ended[:, LANES : 2 * LANES]
        hc = ended[:, 2 * LANES : 3 * LANES]
        far[...] = jnp.zeros((PLANE, LANES), F32)
        later[...] = jnp.zeros((PLANE, LANES), F32)
        pmul[...] = jnp.ones((PLANE, LANES), F32)
        hmul[...] = jnp.ones((PLANE, LANES), F32)

        @pl.when(m == 0)
        def _():
            wait(arecv, ar_sem.at[0])
            theirs = unpack([arecv[j] for j in range(peers)])
            kp, sp = theirs[0:1], theirs[1:2]
            clp, crp = theirs[3:4], theirs[4:5]
            own_left, own_right = leftx[0, me, 1:2, :], rightx[0, me, 1:2, :]
            wall_left, wall_right = pick(leftx, 0, rowp[0], 1), pick(rightx, 0, rowp[1], 1)
            far_left, far_right = pick(leftx, 0, rowp[2], 1), pick(rightx, 0, rowp[3], 1)
            kg = both(at_lane(own_left, 0), at_lane(own_right, 0))
            sg = both(at_lane(own_left, 1), at_lane(own_right, 1))
            ka = both(at_lane(wall_left, 0), at_lane(wall_right, 0))
            kf = both(at_lane(far_left, 0), at_lane(far_right, 0))
            sf = both(at_lane(far_left, 1), at_lane(far_right, 1))
            at_start, at_end = first & has_prev, last & has_next
            clx = jnp.where(at_start, FACE * (k + kg), 0.0)
            crx = jnp.where(at_end, FACE * (k + kg), 0.0)
            cw = jnp.where(jnp.abs(solid - sp) > 0.5, FACE * (k + kp), 0.0)
            cwm = jnp.where(wall_row, cw, 0.0)
            for a in range(N):
                rows_a = slice(a * PLANE, (a + 1) * PLANE)
                extra = cwm + INV_DT
                if a == 0:
                    extra = extra + (clin + clx)
                if a == N - 1:
                    extra = extra + (crin + crx)
                d = RELAX / (extra + k * diag[rows_a, :])
                ds[rows_a, :] = d
                gs[rows_a, :] = 1.0 - d * extra
                dk[rows_a, :] = d * k
                db[rows_a, :] = d * bs[rows_a, :]
            dcl[...] = ds[TOP, :] * clin
            dclh[...] = ds[TOP, :] * clx
            dcr[...] = ds[END, :] * crin
            dcrh[...] = ds[END, :] * crx
            dcw[...] = ds[WALL, :] * cw
            clxp = jnp.where(at_start, FACE * (kp + ka), 0.0)
            crxp = jnp.where(at_end, FACE * (kp + ka), 0.0)
            outer = cw + jnp.where(full_row < N, clxp, 0.0) + jnp.where(full_row >= PLANE - N, crxp, 0.0)
            inner = jnp.where(full_row < N, clp, 0.0) + jnp.where(full_row >= PLANE - N, crp, 0.0)
            dp = RELAX / (INV_DT + kp * diag[WALL, :] + outer + inner)
            far[...] = fx * (1.0 - dp * outer)
            pmul[...] = dp
            dcwp[...] = dp * cw
            dpcl[...] = dp[0:N] * clxp
            dpcr[...] = dp[PLANE - N : PLANE] * crxp
            cxg = clx + crx
            cwg = jnp.where(wall_row, jnp.where(jnp.abs(sg - sf) > 0.5, FACE * (kg + kf), 0.0), 0.0)
            dg = RELAX / (INV_DT + kg * diag[TOP, :] + cxg + cwg)
            later[...] = hb * (1.0 - dg * (cxg + cwg))
            hmul[...] = dg
            dhx[...] = dg * cxg
            dhw[...] = dg * cwg
            local()

        edge = hx[0:PLANE:N, :]
        far[...] += dcwp[...] * xs[WALL, :]
        far[0:N, :] += dpcl[...] * edge
        far[PLANE - N : PLANE, :] += dpcr[...] * edge
        mine = jnp.where(first, xs[TOP, :], xs[END, :])
        later[...] += dhx[...] * mine + dhw[...] * hc

        finish(fx, hb)
        local()

        wait(leftv.at[m], lvr_sem.at[m])
        wait(rightv.at[m], rvr_sem.at[m])
        hv = columns([leftv[m], rightv[m]], end_map[:, 0:LANES])
        wait(wvr.at[m], wvr_sem.at[m])
        fv = unpack([wvr[m, j] for j in range(peers)])
        finish(far[...] + pmul[...] * fv, later[...] + hmul[...] * hv)

        @pl.when(m < PAIRS - 1)
        def _():
            send_x(m + 1)

        @pl.when(m == SWEEPS // 2 - 1)
        def _():
            convect()
            db[...] = ds[...] * bs[...]

        @pl.when(m < PAIRS - 1)
        def _():
            local()
            send_v(m + 1)

        return c

    lax.fori_loop(0, PAIRS, pair, 0)
    out[...] = xs[...]

    wait(asend, as_sem.at[0])
    for m in range(PAIRS):
        wait(wxs.at[m], wxs_sem.at[m])
        wait(wvs.at[m], wvs_sem.at[m])
        wait(leftx.at[m], rx_sem.at[m])
        wait(rightx.at[m], lx_sem.at[m])
        wait(leftv.at[m], rv_sem.at[m])
        wait(rightv.at[m], lv_sem.at[m])


def body(n_sec, n_elem, theta, flow, conduct, metal, patch):
    consts = constants()
    vmem = pl.BlockSpec(memory_space=pltpu.VMEM)

    def block(*shape):
        return pltpu.VMEM(shape, F32)

    field, plane, edge = block(POINTS, LANES), block(PLANE, LANES), block(N, LANES)
    peers = n_sec - 1
    walls = block(PAIRS, peers, HALF, LANES)
    trait = block(peers, HALF, LANES)
    dma = pltpu.SemaphoreType.DMA
    result = pl.pallas_call(
        lambda *refs: kernel(n_sec, n_elem, *refs),
        out_shape=jax.ShapeDtypeStruct((POINTS, LANES), F32),
        in_specs=[vmem] * 9,
        out_specs=vmem,
        scratch_shapes=[field] * 8
        + [
            block(3, N, LANES, LANES),
            block(3, FINE, LANES, LANES),
            block(N, LANES, LANES),
            pltpu.VMEM((LANES, 2 * LANES), BF16),
            block(LANES, LANES),
        ]
        + [plane] * 10 + [edge] * 2 + [plane] * 3
        + [block(4, 1, LANES)] + [walls] * 4 + [trait] * 2
        + [block(PAIRS, 2, 2, LANES), block(PAIRS, 2, 1, LANES)]
        + [block(PAIRS, n_sec, 2, LANES)] * 2
        + [block(PAIRS, 1, LANES)] * 2
        + [dma((PAIRS,))] * 4 + [dma((1,))] * 2 + [dma((PAIRS,))] * 8,
        compiler_params=pltpu.CompilerParams(collective_id=0, has_side_effects=True),
    )(
        theta.reshape(POINTS, LANES),
        flow.reshape(3 * POINTS, LANES),
        conduct, metal, patch,
        *[jnp.asarray(c) for c in consts],
    )
    return result.reshape(theta.shape)


def solution(mesh):
    n_sec, n_elem = mesh.shape["sec"], mesh.shape["elem"]
    return jax.shard_map(
        lambda *args: body(n_sec, n_elem, *args),
        mesh=mesh,
        in_specs=(
            P("sec", None, None, None, "elem"),
            P(None, "sec", None, None, None, "elem"),
            P("sec", "elem"),
            P("sec", "elem"),
            P("sec", "elem"),
        ),
        out_specs=P("sec", None, None, None, "elem"),
        check_vma=False,
    )
```

```python
import jax
import jax.numpy as jnp
import numpy as np
from jax import lax
from jax.experimental import pallas as pl
from jax.experimental.pallas import tpu as pltpu
from jax.sharding import PartitionSpec as P

N = 8
FINE = 11
PLANE = N * N
POINTS = N * N * N
LANES = 128
STEPS = 2
SWEEPS = 4
PAIRS = STEPS * SWEEPS // 2
HALF = 5
ROWS = 8
INV_DT = 20.0
RELAX = 0.4
FAR_FIRST = [d - 1 for d in (10, 6, 2, 14, 9, 11, 7, 5, 13, 3, 15, 1, 8, 4, 12)]
PENALTY = 30.0
MESH = pl.DeviceIdType.MESH
HIGHEST = lax.Precision.HIGHEST
F32 = jnp.float32
BF16 = jnp.bfloat16


def legendre_pair(order, points):
    previous = points * 0.0 + 1.0
    current = points * 1.0
    for level in range(2, order + 1):
        previous, current = (
            current,
            ((2 * level - 1) * points * current - (level - 1) * previous) / level,
        )
    return current, previous


def make_tables():
    degree = N - 1
    x = -np.cos(np.pi * np.arange(N) / degree)
    for _ in range(100):
        cur, prev = legendre_pair(degree, x)
        x = x - (x * cur - prev) / (N * cur)
    values, _ = legendre_pair(degree, x)
    w = 2.0 / (degree * (degree + 1) * values**2)
    dm = np.zeros((N, N))
    for i in range(N):
        for j in range(N):
            if i != j:
                dm[i, j] = values[i] / (values[j] * (x[i] - x[j]))
    dm[0, 0] = -degree * (degree + 1) / 4.0
    dm[-1, -1] = degree * (degree + 1) / 4.0
    g = -np.cos(np.pi * (np.arange(FINE) + 0.75) / (FINE + 0.5))
    for _ in range(100):
        cur, prev = legendre_pair(FINE, g)
        slope = FINE * (g * cur - prev) / (g * g - 1.0)
        g = g - cur / slope
    cur, prev = legendre_pair(FINE, g)
    slope = FINE * (g * cur - prev) / (g * g - 1.0)
    v = 2.0 / ((1.0 - g * g) * slope * slope)
    jm = np.ones((FINE, N))
    for j in range(N):
        for i in range(N):
            if i != j:
                jm[:, j] *= (g - x[i]) / (x[j] - x[i])
    km = dm.T @ (w[:, None] * dm)
    return dm, jm, km, w, v


DM, JM, KM, W, V = make_tables()
JD = JM @ DM
LAP = KM / W[:, None]
ADJ = (JM.T * V[None, :]) / W[:, None]
FACE = PENALTY * 0.5 / W[0]


def halves(m):
    hi = np.asarray(m, np.float32).astype(BF16)
    lo = np.asarray(m - hi.astype(np.float64), np.float32).astype(BF16)
    return hi, lo


def stacked(m):
    hi, lo = halves(m)
    return np.concatenate([hi, hi, lo], axis=1)


def pad_to(m, rows, cols):
    out = np.zeros((rows, cols))
    out[: m.shape[0], : m.shape[1]] = m
    return out


def constants():
    planes = [pad_to(np.kron(p, q), LANES, PLANE) for p, q in ((JM, JM), (JD, JM), (JM, JD))]
    lift = stacked(np.concatenate(planes, axis=0))
    fall = stacked(pad_to(np.kron(ADJ, ADJ), PLANE, LANES))
    eye = np.eye(N)
    flat = np.kron(LAP, eye) + np.kron(eye, LAP)
    main = np.diagonal(LAP)
    diag = main[:, None] + np.diagonal(flat)[None, :]
    diag = np.broadcast_to(diag.reshape(POINTS, 1), (POINTS, LANES)).astype(np.float32)
    return lift, fall, stacked(flat), diag


def dot(a, b):
    return lax.dot_general(a, b, (((1,), (0,)), ((), ())), preferred_element_type=F32)


def dot_nt(a, b):
    return lax.dot_general(a, b, (((1,), (1,)), ((), ())), preferred_element_type=F32)


def split(x):
    hi = x.astype(BF16)
    lo = (x - hi.astype(F32)).astype(BF16)
    return hi, lo


def split3(x):
    hi, lo = split(x)
    return jnp.concatenate([hi, lo, hi], axis=0)


def split_rows(x):
    hi = x.astype(BF16)
    rest = x - hi.astype(F32)
    mid = rest.astype(BF16)
    low = (rest - mid.astype(F32)).astype(BF16)
    return jnp.concatenate([hi.astype(F32), mid.astype(F32), low.astype(F32)], axis=0)


def weighted(coefs, terms):
    total = None
    for c, t in zip(coefs, terms):
        if c == 0.0:
            continue
        total = t * float(c) if total is None else total + t * float(c)
    return total


def up(table, sign, terms):
    even = [terms[a] + terms[7 - a] for a in range(4)]
    odd = [terms[a] - terms[7 - a] for a in range(4)]
    out = [None] * FINE
    for q in range(6):
        ce = [(table[q, a] + table[q, 7 - a]) / 2 for a in range(4)]
        co = [(table[q, a] - table[q, 7 - a]) / 2 for a in range(4)]
        if q == 5:
            out[q] = weighted(ce, even) if sign > 0 else weighted(co, odd)
            continue
        e, o = weighted(ce, even), weighted(co, odd)
        out[q] = e + o
        out[10 - q] = e - o if sign > 0 else o - e
    return out


def across(table, terms):
    even = [terms[j] + terms[7 - j] for j in range(4)]
    odd = [terms[j] - terms[7 - j] for j in range(4)]
    out = [None] * N
    for i in range(4):
        e = weighted([(table[i, j] + table[i, 7 - j]) / 2 for j in range(4)], even)
        o = weighted([(table[i, j] - table[i, 7 - j]) / 2 for j in range(4)], odd)
        out[i] = e + o
        out[7 - i] = e - o
    return out


def down(table, terms):
    even = [terms[q] + terms[10 - q] for q in range(5)] + [terms[5]]
    odd = [terms[q] - terms[10 - q] for q in range(5)]
    out = [None] * N
    for a in range(4):
        ce = [(table[a, q] + table[a, 10 - q]) / 2 for q in range(5)] + [table[a, 5]]
        co = [(table[a, q] - table[a, 10 - q]) / 2 for q in range(5)]
        e, o = weighted(ce, even), weighted(co, odd)
        out[a] = e + o
        out[7 - a] = e - o
    return out


def iota(shape, dim):
    return lax.broadcasted_iota(jnp.int32, shape, dim)


def kernel(
    n_sec, n_elem,
    th, vel_in, kd, mt, pt, lift_in, fall_in, flat_in, diag_in,
    out,
    xs, vs, bs, db, gs, dk, ds, lx, tt, uu, zz, pm, ws,
    far, later, pmul, hmul, dcl, dcr, dclh, dcrh, dcw, dcwp, dpcl, dpcr, dhx, dhw, hx, rowp,
    sfx, shb, sface, smine,
    wxs, wxr, wvs, wvr, asend, arecv, cxs, cvs, leftx, rightx, leftv, rightv, leftc, rightc,
    vel, lift, fall, flat, diag, in_sem,
    wxs_sem, wxr_sem, wvs_sem, wvr_sem, as_sem, ar_sem,
    rx_sem, lx_sem, rv_sem, lv_sem, lxr_sem, rxr_sem, lvr_sem, rvr_sem, rc_sem, lc_sem, lcr_sem, rcr_sem,
):
    me = lax.axis_index("sec")
    el = lax.axis_index("elem")
    nxt = lax.rem(el + 1, n_elem)
    prv = lax.rem(el + n_elem - 1, n_elem)
    peers = n_sec - 1
    TOP = slice(0, PLANE)
    END = slice(POINTS - PLANE, POINTS)
    WALL = slice(0, POINTS, N)

    def sec(d):
        return lax.rem(me + d, n_sec)

    def remote(src, dst, send_sem, recv_sem, to_sec, to_elem):
        pltpu.make_async_remote_copy(
            src, dst, send_sem, recv_sem,
            device_id={"sec": to_sec, "elem": to_elem}, device_id_type=MESH,
        ).start()

    def wait(ref, sem):
        pltpu.make_async_copy(ref, ref, sem).wait()

    barrier = pltpu.get_barrier_semaphore()
    for d in range(n_sec):
        for to in (el, nxt, prv) if d else (nxt, prv):
            pl.semaphore_signal(barrier, inc=1, device_id={"sec": sec(d), "elem": to}, device_id_type=MESH)

    loads = [
        pltpu.make_async_copy(src, dst, in_sem.at[i])
        for i, (src, dst) in enumerate(
            ((vel_in, vel), (lift_in, lift), (th, xs), (fall_in, fall), (flat_in, flat), (diag_in, diag))
        )
    ]
    for load in loads:
        load.start()

    lane = lax.broadcasted_iota(jnp.int32, (1, LANES), 1)
    k = kd[...]
    solid = mt[...].astype(F32)
    patch = pt[...]
    patch_f = patch.astype(F32)
    first, last = lane == 0, lane == LANES - 1
    has_prev = (jnp.zeros((1, LANES), jnp.int32) + el) > 0
    has_next = (jnp.zeros((1, LANES), jnp.int32) + el) < n_elem - 1
    wall_row = lax.rem(iota((PLANE, LANES), 0), N) == 0

    def at_lane(row, i):
        return jnp.sum(jnp.where(lane == i, row, 0.0), axis=1, keepdims=True)

    def rolled(v, by):
        return pltpu.roll(v, by, 1)

    mate = lax.rem(patch - me + n_sec, n_sec) - 1
    member = (iota((16, LANES), 0) == mate).astype(F32)
    before = (iota((LANES, LANES), 0) < iota((LANES, LANES), 1)).astype(F32)
    rank = jnp.sum(member * dot(member, before), axis=0, keepdims=True).astype(jnp.int32)
    slot = iota((LANES, LANES), 0)
    low_slot = ((slot == mate * ROWS + rank) & (rank < HALF)).astype(F32)
    high_slot = ((slot == mate * ROWS + rank - HALF) & (rank >= HALF)).astype(F32)
    pm[...] = jnp.concatenate([low_slot, high_slot], axis=1).astype(BF16)
    ws[...] = jnp.zeros(ws.shape, F32)

    def pack(face):
        total = None
        for piece in split(face):
            none = jnp.zeros_like(piece)
            both = jnp.concatenate(
                [jnp.concatenate([piece, none], axis=1), jnp.concatenate([none, piece], axis=1)], axis=0
            )
            part = dot_nt(pm[...], both)
            total = part if total is None else total + part
        return total

    def unpack(rows):
        for j in range(peers):
            ws[j * ROWS : j * ROWS + HALF, :] = rows[j]
        hi, lo = split(jnp.transpose(ws[...]))
        both = dot(hi, pm[...]) + dot(lo, pm[...])
        return both[0:PLANE, 0:LANES] + both[PLANE : 2 * PLANE, LANES : 2 * LANES]

    clin = jnp.where(first, 0.0, FACE * (k + rolled(k, 1)))
    crin = jnp.where(last, 0.0, FACE * (k + rolled(k, LANES - 1)))

    def lift_planes(src, base, table):
        res = []
        for p in range(4):
            cols = []
            for i in range(2):
                at = base + (2 * p + i) * PLANE
                if not isinstance(at, int):
                    at = pl.multiple_of(at, PLANE)
                cols.append(split3(src[pl.ds(at, PLANE), :]))
            res.append(dot(table, jnp.concatenate(cols, axis=1)))
        return res

    def velocity(d, c):
        for p, r in enumerate(lift_planes(vel, d * POINTS, lift[0:LANES, :])):
            for i in range(2):
                tt[d, 2 * p + i] = r[:, i * LANES : (i + 1) * LANES]
        return c

    loads[0].wait()
    loads[1].wait()
    lax.fori_loop(0, 3, velocity, 0)
    fluid = jnp.broadcast_to(1.0 - solid, (8, LANES))

    def velocity_up(i, c):
        d = i // 16
        rows = pl.ds(pl.multiple_of((i % 16) * 8, 8), 8)
        lifted = up(JM, 1, [tt[d, a, rows, :] for a in range(N)])
        for q in range(FINE):
            uu[d, q, rows, :] = lifted[q] * fluid
        return c

    lax.fori_loop(0, 48, velocity_up, 0, unroll=4)

    def convect():
        for p, r in enumerate(lift_planes(xs, 0, lift[...])):
            for i in range(2):
                for d in range(3):
                    tt[d, 2 * p + i] = r[d * LANES : (d + 1) * LANES, i * LANES : (i + 1) * LANES]

        def product(i, c):
            rows = pl.ds(pl.multiple_of(i * 8, 8), 8)
            total = None
            for d, (table, sign) in enumerate(((JD, -1), (JM, 1), (JM, 1))):
                lifted = up(table, sign, [tt[d, a, rows, :] for a in range(N)])
                terms = [lifted[q] * uu[d, q, rows, :] for q in range(FINE)]
                total = terms if total is None else [x + y for x, y in zip(total, terms)]
            for a, z in enumerate(down(ADJ, total)):
                zz[a, rows, :] = z
            return c

        lax.fori_loop(0, 16, product, 0, unroll=4)
        for p in range(4):
            r = dot(fall[...], jnp.concatenate([split3(zz[2 * p]), split3(zz[2 * p + 1])], axis=1))
            for i in range(2):
                rows = slice((2 * p + i) * PLANE, (2 * p + i + 1) * PLANE)
                bs[rows, :] = INV_DT * xs[rows, :] - r[:, i * LANES : (i + 1) * LANES]

    def laplace(write):
        for p, r in enumerate(lift_planes(xs, 0, flat[...])):
            for i in range(2):
                at = (2 * p + i) * PLANE
                lx[at : at + PLANE, :] = r[:, i * LANES : (i + 1) * LANES]
        for g in range(8):
            rows = [slice(a * PLANE + 8 * g, a * PLANE + 8 * g + 8) for a in range(N)]
            along = across(LAP, [xs[r, :] for r in rows])
            for r, v in zip(rows, along):
                write(r, v + lx[r, :])

    def local():
        def write(r, v):
            vs[r, :] = gs[r, :] * xs[r, :] + db[r, :] - dk[r, :] * v

        laplace(write)
        vs[TOP, :] += dcl[...] * rolled(xs[END, :], 1)
        vs[END, :] += dcr[...] * rolled(xs[TOP, :], LANES - 1)

    corner = iota((16, LANES), 0)
    corner_lane = iota((16, LANES), 1)
    sel_last = jnp.where((corner == 0) & (corner_lane == LANES - 1), 1.0, 0.0).astype(BF16)
    sel_first = jnp.where((corner == 0) & (corner_lane == 0), 1.0, 0.0).astype(BF16)

    def line(sel, plane):
        hi, lo = split(plane)
        both = jnp.concatenate([hi, lo], axis=0)
        r = dot_nt(sel, both)[0:1]
        return r + rolled(r, PLANE)

    def send_x(m):
        packed = pack(xs[WALL, :])
        for j in range(peers):
            wxs[m, j] = packed[j * ROWS : j * ROWS + HALF]
        for j in FAR_FIRST:
            remote(wxs.at[m, j], wxr.at[m, peers - 1 - j], wxs_sem.at[m], wxr_sem.at[m], sec(j + 1), el)
        cxs[m, 0, 0:1] = line(sel_last, xs[END, :])
        cxs[m, 1, 0:1] = line(sel_first, xs[TOP, :])
        remote(cxs.at[m, 0], leftc.at[m], rc_sem.at[m], lcr_sem.at[m], me, nxt)
        remote(cxs.at[m, 1], rightc.at[m], lc_sem.at[m], rcr_sem.at[m], me, prv)
        for d in [j + 1 for j in FAR_FIRST]:
            remote(cxs.at[m, 0], leftx.at[m, d - 1], rx_sem.at[m], lxr_sem.at[m], sec(d), nxt)
            remote(cxs.at[m, 1], rightx.at[m, d - 1], lx_sem.at[m], rxr_sem.at[m], sec(d), prv)

    def send_v(m):
        packed = pack(vs[WALL, :])
        for j in range(peers):
            wvs[m, j] = packed[j * ROWS : j * ROWS + HALF]
        for j in FAR_FIRST:
            remote(wvs.at[m, j], wvr.at[m, peers - 1 - j], wvs_sem.at[m], wvr_sem.at[m], sec(j + 1), el)
        cvs[m, 0] = line(sel_last, vs[END, :])
        cvs[m, 1] = line(sel_first, vs[TOP, :])
        remote(cvs.at[m, 0], leftv.at[m], rv_sem.at[m], lvr_sem.at[m], me, nxt)
        remote(cvs.at[m, 1], rightv.at[m], lv_sem.at[m], rvr_sem.at[m], me, prv)

    for load in loads[2:]:
        load.wait()
    full_row = iota((PLANE, LANES), 0)
    traits = jnp.where(full_row == 0, k, 0.0)
    traits = jnp.where(full_row == 1, solid, traits)
    traits = jnp.where(full_row == 2, patch_f, traits)
    traits = jnp.where(full_row == 3, clin, traits)
    traits = jnp.where(full_row == 4, crin, traits)
    packed_traits = pack(traits)
    for j in range(peers):
        asend[j] = packed_traits[j * ROWS : j * ROWS + HALF]
    cxs[0, 0, 1:2] = line(sel_last, traits)
    cxs[0, 1, 1:2] = line(sel_first, traits)
    for m in range(1, PAIRS):
        for i in range(2):
            cxs[m, i, 1:2] = jnp.zeros((1, LANES), F32)

    pl.semaphore_wait(barrier, 3 * n_sec - 1)
    send_x(0)
    for j in range(peers):
        remote(asend.at[j], arecv.at[peers - 1 - j], as_sem.at[0], ar_sem.at[0], sec(j + 1), el)

    convect()

    def residual(r, v):
        vs[r, :] = bs[r, :] - INV_DT * xs[r, :] - k * v

    laplace(residual)
    vs[TOP, :] += clin * (rolled(xs[END, :], 1) - xs[TOP, :])
    vs[END, :] += crin * (rolled(xs[TOP, :], LANES - 1) - xs[END, :])
    send_v(0)

    row8 = iota((8, LANES), 0)
    lane8 = iota((8, LANES), 1)

    def ends(i):
        return jnp.where(((row8 == i) & (lane8 == 0)) | ((row8 == i + 1) & (lane8 == LANES - 1)), 1.0, 0.0)

    def tripled(m):
        return jnp.concatenate([m] * 3, axis=0).astype(BF16)

    end_map = tripled(jnp.concatenate([ends(0), ends(2)], axis=1))
    me_f = (jnp.zeros((1, 1), jnp.int32) + me).astype(F32)

    def distance(which):
        gap = me_f - which
        return jnp.broadcast_to(jnp.where(gap < 0.0, gap + float(n_sec), gap), (1, LANES))

    def columns(rows, table):
        stack = jnp.zeros((8, LANES), F32)
        for i, r in enumerate(rows):
            stack = jnp.where(row8 == i, r, stack)
        return dot(jnp.transpose(split_rows(stack)).astype(BF16)[0:PLANE], table)

    def pick(ref, m, which, r):
        total = jnp.zeros((1, LANES), F32)
        for q in range(1, n_sec):
            total = jnp.where(which == float(q), ref[m, q - 1, r : r + 1, :], total)
        return total

    def both(at_first, at_last):
        return jnp.where(first, at_first, jnp.where(last, at_last, 0.0))

    def finish(wall, halo):
        xs[...] = vs[...]
        xs[TOP, :] += dclh[...] * halo
        xs[END, :] += dcrh[...] * halo
        xs[WALL, :] += dcw[...] * wall

    def pair(m, c):
        wait(leftc.at[m], lcr_sem.at[m])
        wait(rightc.at[m], rcr_sem.at[m])
        shb[...] = columns([leftc[m, 0:1, :], rightc[m, 0:1, :]], end_map[:, 0:LANES])
        wait(wxr.at[m], wxr_sem.at[m])
        sfx[...] = unpack([wxr[m, j] for j in range(peers)])
        sface[...] = xs[WALL, :]
        smine[...] = jnp.where(first, xs[TOP, :], xs[END, :])
        at_start, at_end = first & has_prev, last & has_next

        @pl.when(m == 0)
        def _():
            wait(arecv, ar_sem.at[0])
            theirs = unpack([arecv[j] for j in range(peers)])
            hx[...] = theirs
            kp, sp = theirs[0:1], theirs[1:2]
            own_left, own_right = leftc[0, 1:2, :], rightc[0, 1:2, :]
            rowp[0] = distance(at_lane(patch_f, 0))
            rowp[1] = distance(at_lane(patch_f, LANES - 1))
            rowp[2] = distance(at_lane(own_left, 2))
            rowp[3] = distance(at_lane(own_right, 2))
            kg = both(at_lane(own_left, 0), at_lane(own_right, 0))
            clx = jnp.where(at_start, FACE * (k + kg), 0.0)
            crx = jnp.where(at_end, FACE * (k + kg), 0.0)
            cw = jnp.where(jnp.abs(solid - sp) > 0.5, FACE * (k + kp), 0.0)
            cwm = jnp.where(wall_row, cw, 0.0)
            for a in range(N):
                rows_a = slice(a * PLANE, (a + 1) * PLANE)
                extra = cwm + INV_DT
                if a == 0:
                    extra = extra + (clin + clx)
                if a == N - 1:
                    extra = extra + (crin + crx)
                d = RELAX / (extra + k * diag[rows_a, :])
                known = INV_DT
                if a == 0:
                    known = known + clin
                if a == N - 1:
                    known = known + crin
                vs[rows_a, :] = xs[rows_a, :] + d * (vs[rows_a, :] - (extra - known) * xs[rows_a, :])
                ds[rows_a, :] = d
                gs[rows_a, :] = 1.0 - d * extra
                dk[rows_a, :] = d * k
                db[rows_a, :] = d * bs[rows_a, :]
            dcl[...] = ds[TOP, :] * clin
            dclh[...] = ds[TOP, :] * clx
            dcr[...] = ds[END, :] * crin
            dcrh[...] = ds[END, :] * crx
            dcw[...] = ds[WALL, :] * cw

        finish(sfx[...], shb[...])
        local()

        wait(leftx.at[m], lxr_sem.at[m])
        wait(rightx.at[m], rxr_sem.at[m])

        @pl.when(m == 0)
        def _():
            kp, sp = hx[0:1, :], hx[1:2, :]
            clp, crp = hx[3:4, :], hx[4:5, :]
            own_left, own_right = leftc[0, 1:2, :], rightc[0, 1:2, :]
            wall_left, wall_right = pick(leftx, 0, rowp[0], 1), pick(rightx, 0, rowp[1], 1)
            far_left, far_right = pick(leftx, 0, rowp[2], 1), pick(rightx, 0, rowp[3], 1)
            kg = both(at_lane(own_left, 0), at_lane(own_right, 0))
            sg = both(at_lane(own_left, 1), at_lane(own_right, 1))
            ka = both(at_lane(wall_left, 0), at_lane(wall_right, 0))
            kf = both(at_lane(far_left, 0), at_lane(far_right, 0))
            sf = both(at_lane(far_left, 1), at_lane(far_right, 1))
            cw = jnp.where(jnp.abs(solid - sp) > 0.5, FACE * (k + kp), 0.0)
            clxp = jnp.where(at_start, FACE * (kp + ka), 0.0)
            crxp = jnp.where(at_end, FACE * (kp + ka), 0.0)
            outer = cw + jnp.where(full_row < N, clxp, 0.0) + jnp.where(full_row >= PLANE - N, crxp, 0.0)
            inner = jnp.where(full_row < N, clp, 0.0) + jnp.where(full_row >= PLANE - N, crp, 0.0)
            dp = RELAX / (INV_DT + kp * diag[WALL, :] + outer + inner)
            far[...] = sfx[...] * (1.0 - dp * outer)
            pmul[...] = dp
            dcwp[...] = dp * cw
            dpcl[...] = dp[0:N] * clxp
            dpcr[...] = dp[PLANE - N : PLANE] * crxp
            cxg = both(jnp.where(at_start, FACE * (k + kg), 0.0), jnp.where(at_end, FACE * (k + kg), 0.0))
            cwg = jnp.where(wall_row, jnp.where(jnp.abs(sg - sf) > 0.5, FACE * (kg + kf), 0.0), 0.0)
            dg = RELAX / (INV_DT + kg * diag[TOP, :] + cxg + cwg)
            later[...] = shb[...] * (1.0 - dg * (cxg + cwg))
            hmul[...] = dg
            dhx[...] = dg * cxg
            dhw[...] = dg * cwg

        @pl.when(m > 0)
        def _():
            far[...] = jnp.zeros((PLANE, LANES), F32)
            later[...] = jnp.zeros((PLANE, LANES), F32)
            pmul[...] = jnp.ones((PLANE, LANES), F32)
            hmul[...] = jnp.ones((PLANE, LANES), F32)

        edges = columns(
            [
                pick(leftx, m, rowp[0], 0), pick(rightx, m, rowp[1], 0),
                pick(leftx, m, rowp[2], 0), pick(rightx, m, rowp[3], 0),
            ],
            end_map,
        )
        hx[...] = edges[:, 0:LANES]
        edge = hx[0:PLANE:N, :]
        far[...] += dcwp[...] * sface[...]
        far[0:N, :] += dpcl[...] * edge
        far[PLANE - N : PLANE, :] += dpcr[...] * edge
        later[...] += dhx[...] * smine[...] + dhw[...] * edges[:, LANES : 2 * LANES]

        wait(leftv.at[m], lvr_sem.at[m])
        wait(rightv.at[m], rvr_sem.at[m])
        hv = columns([leftv[m], rightv[m]], end_map[:, 0:LANES])
        wait(wvr.at[m], wvr_sem.at[m])
        fv = unpack([wvr[m, j] for j in range(peers)])
        finish(far[...] + pmul[...] * fv, later[...] + hmul[...] * hv)

        @pl.when(m < PAIRS - 1)
        def _():
            send_x(m + 1)

        @pl.when(m == SWEEPS // 2 - 1)
        def _():
            convect()
            db[...] = ds[...] * bs[...]

        @pl.when(m < PAIRS - 1)
        def _():
            local()
            send_v(m + 1)

        return c

    lax.fori_loop(0, PAIRS, pair, 0)
    out[...] = xs[...]

    wait(asend, as_sem.at[0])
    for m in range(PAIRS):
        wait(wxs.at[m], wxs_sem.at[m])
        wait(wvs.at[m], wvs_sem.at[m])
        wait(leftx.at[m], rx_sem.at[m])
        wait(rightx.at[m], lx_sem.at[m])
        wait(leftv.at[m], rv_sem.at[m])
        wait(rightv.at[m], lv_sem.at[m])
        wait(leftc.at[m], rc_sem.at[m])
        wait(rightc.at[m], lc_sem.at[m])


def body(n_sec, n_elem, theta, flow, conduct, metal, patch):
    consts = constants()
    vmem = pl.BlockSpec(memory_space=pltpu.VMEM)
    hbm = pl.BlockSpec(memory_space=pl.ANY)

    def block(*shape):
        return pltpu.VMEM(shape, F32)

    field, plane, edge = block(POINTS, LANES), block(PLANE, LANES), block(N, LANES)
    peers = n_sec - 1
    walls = block(PAIRS, peers, HALF, LANES)
    trait = block(peers, HALF, LANES)
    dma = pltpu.SemaphoreType.DMA
    result = pl.pallas_call(
        lambda *refs: kernel(n_sec, n_elem, *refs),
        out_shape=jax.ShapeDtypeStruct((POINTS, LANES), F32),
        in_specs=[hbm] * 2 + [vmem] * 3 + [hbm] * 4,
        out_specs=vmem,
        scratch_shapes=[field] * 8
        + [
            block(3, N, LANES, LANES),
            block(3, FINE, LANES, LANES),
            block(N, LANES, LANES),
            pltpu.VMEM((LANES, 2 * LANES), BF16),
            block(LANES, LANES),
        ]
        + [plane] * 10 + [edge] * 2 + [plane] * 3
        + [block(4, 1, LANES)] + [plane] * 4 + [walls] * 4 + [trait] * 2
        + [block(PAIRS, 2, 2, LANES), block(PAIRS, 2, 1, LANES)]
        + [block(PAIRS, peers, 2, LANES)] * 2
        + [block(PAIRS, 1, LANES)] * 2
        + [block(PAIRS, 2, LANES)] * 2
        + [block(3 * POINTS, LANES)]
        + [pltpu.VMEM(c.shape, BF16) for c in consts[:3]]
        + [field, dma((6,))]
        + [dma((PAIRS,))] * 4 + [dma((1,))] * 2 + [dma((PAIRS,))] * 12,
        compiler_params=pltpu.CompilerParams(collective_id=0, has_side_effects=True),
    )(
        theta.reshape(POINTS, LANES),
        flow.reshape(3 * POINTS, LANES),
        conduct, metal, patch,
        *[jnp.asarray(c) for c in consts],
    )
    return result.reshape(theta.shape)


def solution(mesh):
    n_sec, n_elem = mesh.shape["sec"], mesh.shape["elem"]
    return jax.shard_map(
        lambda *args: body(n_sec, n_elem, *args),
        mesh=mesh,
        in_specs=(
            P("sec", None, None, None, "elem"),
            P(None, "sec", None, None, None, "elem"),
            P("sec", "elem"),
            P("sec", "elem"),
            P("sec", "elem"),
        ),
        out_specs=P("sec", None, None, None, "elem"),
        check_vma=False,
    )
```

```python
import jax
import jax.numpy as jnp
import numpy as np
from jax import lax
from jax.experimental import pallas as pl
from jax.experimental.pallas import tpu as pltpu
from jax.sharding import PartitionSpec as P

N = 8
FINE = 11
PLANE = N * N
POINTS = N * N * N
LANES = 128
STEPS = 2
SWEEPS = 4
PAIRS = STEPS * SWEEPS // 2
HALF = 5
ROWS = 8
INV_DT = 20.0
RELAX = 0.4
FAR_FIRST = [d - 1 for d in (10, 6, 2, 14, 9, 11, 7, 5, 13, 3, 15, 1, 8, 4, 12)]
PENALTY = 30.0
MESH = pl.DeviceIdType.MESH
HIGHEST = lax.Precision.HIGHEST
F32 = jnp.float32
BF16 = jnp.bfloat16


def legendre_pair(order, points):
    previous = points * 0.0 + 1.0
    current = points * 1.0
    for level in range(2, order + 1):
        previous, current = (
            current,
            ((2 * level - 1) * points * current - (level - 1) * previous) / level,
        )
    return current, previous


def make_tables():
    degree = N - 1
    x = -np.cos(np.pi * np.arange(N) / degree)
    for _ in range(100):
        cur, prev = legendre_pair(degree, x)
        x = x - (x * cur - prev) / (N * cur)
    values, _ = legendre_pair(degree, x)
    w = 2.0 / (degree * (degree + 1) * values**2)
    dm = np.zeros((N, N))
    for i in range(N):
        for j in range(N):
            if i != j:
                dm[i, j] = values[i] / (values[j] * (x[i] - x[j]))
    dm[0, 0] = -degree * (degree + 1) / 4.0
    dm[-1, -1] = degree * (degree + 1) / 4.0
    g = -np.cos(np.pi * (np.arange(FINE) + 0.75) / (FINE + 0.5))
    for _ in range(100):
        cur, prev = legendre_pair(FINE, g)
        slope = FINE * (g * cur - prev) / (g * g - 1.0)
        g = g - cur / slope
    cur, prev = legendre_pair(FINE, g)
    slope = FINE * (g * cur - prev) / (g * g - 1.0)
    v = 2.0 / ((1.0 - g * g) * slope * slope)
    jm = np.ones((FINE, N))
    for j in range(N):
        for i in range(N):
            if i != j:
                jm[:, j] *= (g - x[i]) / (x[j] - x[i])
    km = dm.T @ (w[:, None] * dm)
    return dm, jm, km, w, v


DM, JM, KM, W, V = make_tables()
JD = JM @ DM
LAP = KM / W[:, None]
ADJ = (JM.T * V[None, :]) / W[:, None]
FACE = PENALTY * 0.5 / W[0]


def halves(m):
    hi = np.asarray(m, np.float32).astype(BF16)
    lo = np.asarray(m - hi.astype(np.float64), np.float32).astype(BF16)
    return hi, lo


def stacked(m):
    hi, lo = halves(m)
    return np.concatenate([hi, hi, lo], axis=1)


def pad_to(m, rows, cols):
    out = np.zeros((rows, cols))
    out[: m.shape[0], : m.shape[1]] = m
    return out


def constants():
    planes = [pad_to(np.kron(p, q), LANES, PLANE) for p, q in ((JM, JM), (JD, JM), (JM, JD))]
    lift = stacked(np.concatenate(planes, axis=0))
    fall = stacked(pad_to(np.kron(ADJ, ADJ), PLANE, LANES))
    eye = np.eye(N)
    flat = np.kron(LAP, eye) + np.kron(eye, LAP)
    main = np.diagonal(LAP)
    diag = main[:, None] + np.diagonal(flat)[None, :]
    diag = np.broadcast_to(diag.reshape(POINTS, 1), (POINTS, LANES)).astype(np.float32)
    return lift, fall, stacked(flat), diag


def dot(a, b):
    return lax.dot_general(a, b, (((1,), (0,)), ((), ())), preferred_element_type=F32)


def dot_nt(a, b):
    return lax.dot_general(a, b, (((1,), (1,)), ((), ())), preferred_element_type=F32)


def split(x):
    hi = x.astype(BF16)
    lo = (x - hi.astype(F32)).astype(BF16)
    return hi, lo


def split3(x):
    hi, lo = split(x)
    return jnp.concatenate([hi, lo, hi], axis=0)


def split_rows(x):
    hi = x.astype(BF16)
    rest = x - hi.astype(F32)
    mid = rest.astype(BF16)
    low = (rest - mid.astype(F32)).astype(BF16)
    return jnp.concatenate([hi.astype(F32), mid.astype(F32), low.astype(F32)], axis=0)


def weighted(coefs, terms):
    total = None
    for c, t in zip(coefs, terms):
        if c == 0.0:
            continue
        total = t * float(c) if total is None else total + t * float(c)
    return total


def up(table, sign, terms):
    even = [terms[a] + terms[7 - a] for a in range(4)]
    odd = [terms[a] - terms[7 - a] for a in range(4)]
    out = [None] * FINE
    for q in range(6):
        ce = [(table[q, a] + table[q, 7 - a]) / 2 for a in range(4)]
        co = [(table[q, a] - table[q, 7 - a]) / 2 for a in range(4)]
        if q == 5:
            out[q] = weighted(ce, even) if sign > 0 else weighted(co, odd)
            continue
        e, o = weighted(ce, even), weighted(co, odd)
        out[q] = e + o
        out[10 - q] = e - o if sign > 0 else o - e
    return out


def across(table, terms):
    even = [terms[j] + terms[7 - j] for j in range(4)]
    odd = [terms[j] - terms[7 - j] for j in range(4)]
    out = [None] * N
    for i in range(4):
        e = weighted([(table[i, j] + table[i, 7 - j]) / 2 for j in range(4)], even)
        o = weighted([(table[i, j] - table[i, 7 - j]) / 2 for j in range(4)], odd)
        out[i] = e + o
        out[7 - i] = e - o
    return out


def down(table, terms):
    even = [terms[q] + terms[10 - q] for q in range(5)] + [terms[5]]
    odd = [terms[q] - terms[10 - q] for q in range(5)]
    out = [None] * N
    for a in range(4):
        ce = [(table[a, q] + table[a, 10 - q]) / 2 for q in range(5)] + [table[a, 5]]
        co = [(table[a, q] - table[a, 10 - q]) / 2 for q in range(5)]
        e, o = weighted(ce, even), weighted(co, odd)
        out[a] = e + o
        out[7 - a] = e - o
    return out


def iota(shape, dim):
    return lax.broadcasted_iota(jnp.int32, shape, dim)


def kernel(
    n_sec, n_elem,
    th, vel_in, kd, mt, pt, lift_in, fall_in, flat_in, diag_in,
    out,
    xs, vs, bs, db, gs, dk, ds, lx, tt, uu, zz, pm, ws,
    far, later, pmul, hmul, dcl, dcr, dclh, dcrh, dcw, dcwp, dpcl, dpcr, dhx, dhw, hx, rowp,
    sfx, shb, sface, smine,
    wxs, wxr, wvs, wvr, asend, arecv, cxs, cvs, leftx, rightx, leftv, rightv, leftc, rightc,
    vel, lift, fall, flat, diag, in_sem,
    wxs_sem, wxr_sem, wvs_sem, wvr_sem, as_sem, ar_sem,
    rx_sem, lx_sem, rv_sem, lv_sem, lxr_sem, rxr_sem, lvr_sem, rvr_sem, rc_sem, lc_sem, lcr_sem, rcr_sem,
):
    me = lax.axis_index("sec")
    el = lax.axis_index("elem")
    nxt = lax.rem(el + 1, n_elem)
    prv = lax.rem(el + n_elem - 1, n_elem)
    peers = n_sec - 1
    TOP = slice(0, PLANE)
    END = slice(POINTS - PLANE, POINTS)
    WALL = slice(0, POINTS, N)

    def sec(d):
        return lax.rem(me + d, n_sec)

    def remote(src, dst, send_sem, recv_sem, to_sec, to_elem):
        pltpu.make_async_remote_copy(
            src, dst, send_sem, recv_sem,
            device_id={"sec": to_sec, "elem": to_elem}, device_id_type=MESH,
        ).start()

    def wait(ref, sem):
        pltpu.make_async_copy(ref, ref, sem).wait()

    barrier = pltpu.get_barrier_semaphore()
    for d in range(n_sec):
        for to in (el, nxt, prv) if d else (nxt, prv):
            pl.semaphore_signal(barrier, inc=1, device_id={"sec": sec(d), "elem": to}, device_id_type=MESH)

    loads = [
        pltpu.make_async_copy(src, dst, in_sem.at[i])
        for i, (src, dst) in enumerate(
            ((vel_in, vel), (lift_in, lift), (th, xs), (fall_in, fall), (flat_in, flat), (diag_in, diag))
        )
    ]
    for load in loads:
        load.start()

    lane = lax.broadcasted_iota(jnp.int32, (1, LANES), 1)
    k = kd[...]
    solid = mt[...].astype(F32)
    patch = pt[...]
    patch_f = patch.astype(F32)
    first, last = lane == 0, lane == LANES - 1
    has_prev = (jnp.zeros((1, LANES), jnp.int32) + el) > 0
    has_next = (jnp.zeros((1, LANES), jnp.int32) + el) < n_elem - 1
    wall_row = lax.rem(iota((PLANE, LANES), 0), N) == 0

    def at_lane(row, i):
        return jnp.sum(jnp.where(lane == i, row, 0.0), axis=1, keepdims=True)

    def rolled(v, by):
        return pltpu.roll(v, by, 1)

    mate = lax.rem(patch - me + n_sec, n_sec) - 1
    member = (iota((16, LANES), 0) == mate).astype(F32)
    before = (iota((LANES, LANES), 0) < iota((LANES, LANES), 1)).astype(F32)
    rank = jnp.sum(member * dot(member, before), axis=0, keepdims=True).astype(jnp.int32)
    slot = iota((LANES, LANES), 0)
    low_slot = ((slot == mate * ROWS + rank) & (rank < HALF)).astype(F32)
    high_slot = ((slot == mate * ROWS + rank - HALF) & (rank >= HALF)).astype(F32)
    pm[...] = jnp.concatenate([low_slot, high_slot], axis=1).astype(BF16)
    ws[...] = jnp.zeros(ws.shape, F32)

    def pack(face):
        total = None
        for piece in split(face):
            none = jnp.zeros_like(piece)
            both = jnp.concatenate(
                [jnp.concatenate([piece, none], axis=1), jnp.concatenate([none, piece], axis=1)], axis=0
            )
            part = dot_nt(pm[...], both)
            total = part if total is None else total + part
        return total

    def unpack(rows):
        for j in range(peers):
            ws[j * ROWS : j * ROWS + HALF, :] = rows[j]
        hi, lo = split(jnp.transpose(ws[...]))
        both = dot(hi, pm[...]) + dot(lo, pm[...])
        return both[0:PLANE, 0:LANES] + both[PLANE : 2 * PLANE, LANES : 2 * LANES]

    clin = jnp.where(first, 0.0, FACE * (k + rolled(k, 1)))
    crin = jnp.where(last, 0.0, FACE * (k + rolled(k, LANES - 1)))

    def lift_planes(src, base, table):
        res = []
        for p in range(4):
            cols = []
            for i in range(2):
                at = base + (2 * p + i) * PLANE
                if not isinstance(at, int):
                    at = pl.multiple_of(at, PLANE)
                cols.append(split3(src[pl.ds(at, PLANE), :]))
            res.append(dot(table, jnp.concatenate(cols, axis=1)))
        return res

    def velocity(d, c):
        for p, r in enumerate(lift_planes(vel, d * POINTS, lift[0:LANES, :])):
            for i in range(2):
                tt[d, 2 * p + i] = r[:, i * LANES : (i + 1) * LANES]
        return c

    loads[0].wait()
    loads[1].wait()
    lax.fori_loop(0, 3, velocity, 0)
    fluid = jnp.broadcast_to(1.0 - solid, (8, LANES))

    def velocity_up(i, c):
        d = i // 16
        rows = pl.ds(pl.multiple_of((i % 16) * 8, 8), 8)
        lifted = up(JM, 1, [tt[d, a, rows, :] for a in range(N)])
        for q in range(FINE):
            uu[d, q, rows, :] = lifted[q] * fluid
        return c

    lax.fori_loop(0, 48, velocity_up, 0, unroll=4)

    def convect():
        for p, r in enumerate(lift_planes(xs, 0, lift[...])):
            for i in range(2):
                for d in range(3):
                    tt[d, 2 * p + i] = r[d * LANES : (d + 1) * LANES, i * LANES : (i + 1) * LANES]

        def product(i, c):
            rows = pl.ds(pl.multiple_of(i * 8, 8), 8)
            total = None
            for d, (table, sign) in enumerate(((JD, -1), (JM, 1), (JM, 1))):
                lifted = up(table, sign, [tt[d, a, rows, :] for a in range(N)])
                terms = [lifted[q] * uu[d, q, rows, :] for q in range(FINE)]
                total = terms if total is None else [x + y for x, y in zip(total, terms)]
            for a, z in enumerate(down(ADJ, total)):
                zz[a, rows, :] = z
            return c

        lax.fori_loop(0, 16, product, 0, unroll=4)
        for p in range(4):
            r = dot(fall[...], jnp.concatenate([split3(zz[2 * p]), split3(zz[2 * p + 1])], axis=1))
            for i in range(2):
                rows = slice((2 * p + i) * PLANE, (2 * p + i + 1) * PLANE)
                bs[rows, :] = INV_DT * xs[rows, :] - r[:, i * LANES : (i + 1) * LANES]

    def laplace(write):
        for p, r in enumerate(lift_planes(xs, 0, flat[...])):
            for i in range(2):
                at = (2 * p + i) * PLANE
                lx[at : at + PLANE, :] = r[:, i * LANES : (i + 1) * LANES]
        for g in range(8):
            rows = [slice(a * PLANE + 8 * g, a * PLANE + 8 * g + 8) for a in range(N)]
            along = across(LAP, [xs[r, :] for r in rows])
            for r, v in zip(rows, along):
                write(r, v + lx[r, :])

    def local():
        def write(r, v):
            vs[r, :] = gs[r, :] * xs[r, :] + db[r, :] - dk[r, :] * v

        laplace(write)
        vs[TOP, :] += dcl[...] * rolled(xs[END, :], 1)
        vs[END, :] += dcr[...] * rolled(xs[TOP, :], LANES - 1)

    corner = iota((16, LANES), 0)
    corner_lane = iota((16, LANES), 1)
    sel_last = jnp.where((corner == 0) & (corner_lane == LANES - 1), 1.0, 0.0).astype(BF16)
    sel_first = jnp.where((corner == 0) & (corner_lane == 0), 1.0, 0.0).astype(BF16)

    def line(sel, plane):
        hi, lo = split(plane)
        both = jnp.concatenate([hi, lo], axis=0)
        r = dot_nt(sel, both)[0:1]
        return r + rolled(r, PLANE)

    def send_x(m):
        packed = pack(xs[WALL, :])
        for j in range(peers):
            wxs[m, j] = packed[j * ROWS : j * ROWS + HALF]
        for j in FAR_FIRST:
            remote(wxs.at[m, j], wxr.at[m, peers - 1 - j], wxs_sem.at[m], wxr_sem.at[m], sec(j + 1), el)
        cxs[m, 0, 0:1] = line(sel_last, xs[END, :])
        cxs[m, 1, 0:1] = line(sel_first, xs[TOP, :])
        remote(cxs.at[m, 0], leftc.at[m], rc_sem.at[m], lcr_sem.at[m], me, nxt)
        remote(cxs.at[m, 1], rightc.at[m], lc_sem.at[m], rcr_sem.at[m], me, prv)
        for d in [j + 1 for j in FAR_FIRST]:
            remote(cxs.at[m, 0], leftx.at[m, d - 1], rx_sem.at[m], lxr_sem.at[m], sec(d), nxt)
            remote(cxs.at[m, 1], rightx.at[m, d - 1], lx_sem.at[m], rxr_sem.at[m], sec(d), prv)

    def send_v(m):
        packed = pack(vs[WALL, :])
        for j in range(peers):
            wvs[m, j] = packed[j * ROWS : j * ROWS + HALF]
        for j in FAR_FIRST:
            remote(wvs.at[m, j], wvr.at[m, peers - 1 - j], wvs_sem.at[m], wvr_sem.at[m], sec(j + 1), el)
        cvs[m, 0] = line(sel_last, vs[END, :])
        cvs[m, 1] = line(sel_first, vs[TOP, :])
        remote(cvs.at[m, 0], leftv.at[m], rv_sem.at[m], lvr_sem.at[m], me, nxt)
        remote(cvs.at[m, 1], rightv.at[m], lv_sem.at[m], rvr_sem.at[m], me, prv)

    for load in loads[2:]:
        load.wait()
    full_row = iota((PLANE, LANES), 0)
    traits = jnp.where(full_row == 0, k, 0.0)
    traits = jnp.where(full_row == 1, solid, traits)
    traits = jnp.where(full_row == 2, patch_f, traits)
    traits = jnp.where(full_row == 3, clin, traits)
    traits = jnp.where(full_row == 4, crin, traits)
    packed_traits = pack(traits)
    for j in range(peers):
        asend[j] = packed_traits[j * ROWS : j * ROWS + HALF]
    cxs[0, 0, 1:2] = line(sel_last, traits)
    cxs[0, 1, 1:2] = line(sel_first, traits)
    for m in range(1, PAIRS):
        for i in range(2):
            cxs[m, i, 1:2] = jnp.zeros((1, LANES), F32)

    pl.semaphore_wait(barrier, 3 * n_sec - 1)
    send_x(0)
    for j in range(peers):
        remote(asend.at[j], arecv.at[peers - 1 - j], as_sem.at[0], ar_sem.at[0], sec(j + 1), el)

    convect()

    def residual(r, v):
        vs[r, :] = bs[r, :] - INV_DT * xs[r, :] - k * v

    laplace(residual)
    vs[TOP, :] += clin * (rolled(xs[END, :], 1) - xs[TOP, :])
    vs[END, :] += crin * (rolled(xs[TOP, :], LANES - 1) - xs[END, :])
    send_v(0)

    row8 = iota((8, LANES), 0)
    lane8 = iota((8, LANES), 1)

    def ends(i):
        return jnp.where(((row8 == i) & (lane8 == 0)) | ((row8 == i + 1) & (lane8 == LANES - 1)), 1.0, 0.0)

    def tripled(m):
        return jnp.concatenate([m] * 3, axis=0).astype(BF16)

    end_map = tripled(jnp.concatenate([ends(0), ends(2)], axis=1))
    me_f = (jnp.zeros((1, 1), jnp.int32) + me).astype(F32)

    def distance(which):
        gap = me_f - which
        return jnp.broadcast_to(jnp.where(gap < 0.0, gap + float(n_sec), gap), (1, LANES))

    def columns(rows, table):
        stack = jnp.zeros((8, LANES), F32)
        for i, r in enumerate(rows):
            stack = jnp.where(row8 == i, r, stack)
        return dot(jnp.transpose(split_rows(stack)).astype(BF16)[0:PLANE], table)

    def pick(ref, m, which, r):
        total = jnp.zeros((1, LANES), F32)
        for q in range(1, n_sec):
            total = jnp.where(which == float(q), ref[m, q - 1, r : r + 1, :], total)
        return total

    def both(at_first, at_last):
        return jnp.where(first, at_first, jnp.where(last, at_last, 0.0))

    def finish(wall, halo):
        xs[...] = vs[...]
        xs[TOP, :] += dclh[...] * halo
        xs[END, :] += dcrh[...] * halo
        xs[WALL, :] += dcw[...] * wall

    def pair(m, c):
        wait(leftc.at[m], lcr_sem.at[m])
        wait(rightc.at[m], rcr_sem.at[m])
        shb[...] = columns([leftc[m, 0:1, :], rightc[m, 0:1, :]], end_map[:, 0:LANES])
        wait(wxr.at[m], wxr_sem.at[m])
        sfx[...] = unpack([wxr[m, j] for j in range(peers)])
        sface[...] = xs[WALL, :]
        smine[...] = jnp.where(first, xs[TOP, :], xs[END, :])
        at_start, at_end = first & has_prev, last & has_next

        @pl.when(m == 0)
        def _():
            wait(arecv, ar_sem.at[0])
            theirs = unpack([arecv[j] for j in range(peers)])
            hx[...] = theirs
            kp, sp = theirs[0:1], theirs[1:2]
            own_left, own_right = leftc[0, 1:2, :], rightc[0, 1:2, :]
            rowp[0] = distance(at_lane(patch_f, 0))
            rowp[1] = distance(at_lane(patch_f, LANES - 1))
            rowp[2] = distance(at_lane(own_left, 2))
            rowp[3] = distance(at_lane(own_right, 2))
            kg = both(at_lane(own_left, 0), at_lane(own_right, 0))
            clx = jnp.where(at_start, FACE * (k + kg), 0.0)
            crx = jnp.where(at_end, FACE * (k + kg), 0.0)
            cw = jnp.where(jnp.abs(solid - sp) > 0.5, FACE * (k + kp), 0.0)
            cwm = jnp.where(wall_row, cw, 0.0)
            for a in range(N):
                rows_a = slice(a * PLANE, (a + 1) * PLANE)
                extra = cwm + INV_DT
                if a == 0:
                    extra = extra + (clin + clx)
                if a == N - 1:
                    extra = extra + (crin + crx)
                d = RELAX / (extra + k * diag[rows_a, :])
                known = INV_DT
                if a == 0:
                    known = known + clin
                if a == N - 1:
                    known = known + crin
                vs[rows_a, :] = xs[rows_a, :] + d * (vs[rows_a, :] - (extra - known) * xs[rows_a, :])
                ds[rows_a, :] = d
                gs[rows_a, :] = 1.0 - d * extra
                dk[rows_a, :] = d * k
                db[rows_a, :] = d * bs[rows_a, :]
            dcl[...] = ds[TOP, :] * clin
            dclh[...] = ds[TOP, :] * clx
            dcr[...] = ds[END, :] * crin
            dcrh[...] = ds[END, :] * crx
            dcw[...] = ds[WALL, :] * cw

        finish(sfx[...], shb[...])
        local()

        wait(leftx.at[m], lxr_sem.at[m])
        wait(rightx.at[m], rxr_sem.at[m])

        @pl.when(m == 0)
        def _():
            kp, sp = hx[0:1, :], hx[1:2, :]
            clp, crp = hx[3:4, :], hx[4:5, :]
            own_left, own_right = leftc[0, 1:2, :], rightc[0, 1:2, :]
            wall_left, wall_right = pick(leftx, 0, rowp[0], 1), pick(rightx, 0, rowp[1], 1)
            far_left, far_right = pick(leftx, 0, rowp[2], 1), pick(rightx, 0, rowp[3], 1)
            kg = both(at_lane(own_left, 0), at_lane(own_right, 0))
            sg = both(at_lane(own_left, 1), at_lane(own_right, 1))
            ka = both(at_lane(wall_left, 0), at_lane(wall_right, 0))
            kf = both(at_lane(far_left, 0), at_lane(far_right, 0))
            sf = both(at_lane(far_left, 1), at_lane(far_right, 1))
            cw = jnp.where(jnp.abs(solid - sp) > 0.5, FACE * (k + kp), 0.0)
            clxp = jnp.where(at_start, FACE * (kp + ka), 0.0)
            crxp = jnp.where(at_end, FACE * (kp + ka), 0.0)
            outer = cw + jnp.where(full_row < N, clxp, 0.0) + jnp.where(full_row >= PLANE - N, crxp, 0.0)
            inner = jnp.where(full_row < N, clp, 0.0) + jnp.where(full_row >= PLANE - N, crp, 0.0)
            dp = RELAX / (INV_DT + kp * diag[WALL, :] + outer + inner)
            far[...] = sfx[...] * (1.0 - dp * outer)
            pmul[...] = dp
            dcwp[...] = dp * cw
            dpcl[...] = dp[0:N] * clxp
            dpcr[...] = dp[PLANE - N : PLANE] * crxp
            cxg = both(jnp.where(at_start, FACE * (k + kg), 0.0), jnp.where(at_end, FACE * (k + kg), 0.0))
            cwg = jnp.where(wall_row, jnp.where(jnp.abs(sg - sf) > 0.5, FACE * (kg + kf), 0.0), 0.0)
            dg = RELAX / (INV_DT + kg * diag[TOP, :] + cxg + cwg)
            later[...] = shb[...] * (1.0 - dg * (cxg + cwg))
            hmul[...] = dg
            dhx[...] = dg * cxg
            dhw[...] = dg * cwg

        @pl.when(m > 0)
        def _():
            far[...] = jnp.zeros((PLANE, LANES), F32)
            later[...] = jnp.zeros((PLANE, LANES), F32)
            pmul[...] = jnp.ones((PLANE, LANES), F32)
            hmul[...] = jnp.ones((PLANE, LANES), F32)

        edges = columns(
            [
                pick(leftx, m, rowp[0], 0), pick(rightx, m, rowp[1], 0),
                pick(leftx, m, rowp[2], 0), pick(rightx, m, rowp[3], 0),
            ],
            end_map,
        )
        hx[...] = edges[:, 0:LANES]
        edge = hx[0:PLANE:N, :]
        far[...] += dcwp[...] * sface[...]
        far[0:N, :] += dpcl[...] * edge
        far[PLANE - N : PLANE, :] += dpcr[...] * edge
        later[...] += dhx[...] * smine[...] + dhw[...] * edges[:, LANES : 2 * LANES]

        wait(leftv.at[m], lvr_sem.at[m])
        wait(rightv.at[m], rvr_sem.at[m])
        hv = columns([leftv[m], rightv[m]], end_map[:, 0:LANES])
        wait(wvr.at[m], wvr_sem.at[m])
        fv = unpack([wvr[m, j] for j in range(peers)])
        finish(far[...] + pmul[...] * fv, later[...] + hmul[...] * hv)

        @pl.when(m < PAIRS - 1)
        def _():
            send_x(m + 1)

        @pl.when(m == SWEEPS // 2 - 1)
        def _():
            convect()
            db[...] = ds[...] * bs[...]

        @pl.when(m < PAIRS - 1)
        def _():
            local()
            send_v(m + 1)

        return c

    for step in range(PAIRS):
        pair(step, 0)
    out[...] = xs[...]

    wait(asend, as_sem.at[0])
    for m in range(PAIRS):
        wait(wxs.at[m], wxs_sem.at[m])
        wait(wvs.at[m], wvs_sem.at[m])
        wait(leftx.at[m], rx_sem.at[m])
        wait(rightx.at[m], lx_sem.at[m])
        wait(leftv.at[m], rv_sem.at[m])
        wait(rightv.at[m], lv_sem.at[m])
        wait(leftc.at[m], rc_sem.at[m])
        wait(rightc.at[m], lc_sem.at[m])


def body(n_sec, n_elem, theta, flow, conduct, metal, patch):
    consts = constants()
    vmem = pl.BlockSpec(memory_space=pltpu.VMEM)
    hbm = pl.BlockSpec(memory_space=pl.ANY)

    def block(*shape):
        return pltpu.VMEM(shape, F32)

    field, plane, edge = block(POINTS, LANES), block(PLANE, LANES), block(N, LANES)
    peers = n_sec - 1
    walls = block(PAIRS, peers, HALF, LANES)
    trait = block(peers, HALF, LANES)
    dma = pltpu.SemaphoreType.DMA
    result = pl.pallas_call(
        lambda *refs: kernel(n_sec, n_elem, *refs),
        out_shape=jax.ShapeDtypeStruct((POINTS, LANES), F32),
        in_specs=[hbm] * 2 + [vmem] * 3 + [hbm] * 4,
        out_specs=vmem,
        scratch_shapes=[field] * 8
        + [
            block(3, N, LANES, LANES),
            block(3, FINE, LANES, LANES),
            block(N, LANES, LANES),
            pltpu.VMEM((LANES, 2 * LANES), BF16),
            block(LANES, LANES),
        ]
        + [plane] * 10 + [edge] * 2 + [plane] * 3
        + [block(4, 1, LANES)] + [plane] * 4 + [walls] * 4 + [trait] * 2
        + [block(PAIRS, 2, 2, LANES), block(PAIRS, 2, 1, LANES)]
        + [block(PAIRS, peers, 2, LANES)] * 2
        + [block(PAIRS, 1, LANES)] * 2
        + [block(PAIRS, 2, LANES)] * 2
        + [block(3 * POINTS, LANES)]
        + [pltpu.VMEM(c.shape, BF16) for c in consts[:3]]
        + [field, dma((6,))]
        + [dma((PAIRS,))] * 4 + [dma((1,))] * 2 + [dma((PAIRS,))] * 12,
        compiler_params=pltpu.CompilerParams(collective_id=0, has_side_effects=True),
    )(
        theta.reshape(POINTS, LANES),
        flow.reshape(3 * POINTS, LANES),
        conduct, metal, patch,
        *[jnp.asarray(c) for c in consts],
    )
    return result.reshape(theta.shape)


def solution(mesh):
    n_sec, n_elem = mesh.shape["sec"], mesh.shape["elem"]
    return jax.shard_map(
        lambda *args: body(n_sec, n_elem, *args),
        mesh=mesh,
        in_specs=(
            P("sec", None, None, None, "elem"),
            P(None, "sec", None, None, None, "elem"),
            P("sec", "elem"),
            P("sec", "elem"),
            P("sec", "elem"),
        ),
        out_specs=P("sec", None, None, None, "elem"),
        check_vma=False,
    )
```
